256 devices in a mesh: img: 32 (over y, z), grp: 8 (over x, core).
Axes of the slice: x: 4, y: 4, z: 8, core: 2. Of those that a mesh axis runs over, the one named last changes fastest.
Arguments:
- images: bfloat16 [8192, 128, 512], P(('img', 'grp')), may hold values from -18 to 18
- group_ids: int32 [8192], P(('img', 'grp')), may hold values from 0 to 7
- counts: int32 [128], replicated, may hold values from 1 to 128, as said below
- radial_basis: bfloat16 [128, 128, 128], replicated, may hold values from -0.5 to 0.5
- ctf_gain: float32 [8, 128], replicated, may hold values from 0.2 to 2
- noise_var: float32 [128], replicated, may hold values from 0.25 to 2
Outputs:
- denoised: bfloat16 [8192, 128, 512], P(('img', 'grp'))
The draws below stay inside these ranges and needn't reach their ends.
Inputs may be any that keep to these rules, and one draw needn't show every extreme that they name: In every aligned block of 4 frequencies the counts sum to exactly 320 and the largest is exactly 128.
All inputs are finite; a program needn't handle non-finite values.
Results may differ from the reference program's by a relative error of at most 0.0063.
The reference program's roundings to bfloat16 on the way (of `basis_used`, `spectrum`, `coeffs`, `scaled`, `filters`, `cleaned` and `back`) count: a program that leaves them out, or rounds other values in their place, can miss the bound.
Values may be sent and summed in bfloat16 or wider, within the bound.
A program may use at most 128 MiB of HBM per device.

```python
import math
import jax
import jax.numpy as jnp
from jax import lax

R = 128
A = 512
K = 128
PMAX = 128
G = 8
NS_ITERS = 7
IMG_DEV = 32
IMAGES = 8192
OWNED = 4
SLOTS = 320
N_GRP = 8


def draw_images(key, part):
    image_index = jnp.arange(IMAGES, dtype=jnp.int32)
    column = image_index // IMG_DEV % N_GRP
    power = column.astype(jnp.float32) / (N_GRP - 1.0)
    amplitude = jnp.exp(power * jnp.log(3.0))
    values = jnp.clip(jax.random.normal(key, (IMAGES, R, A), jnp.float32), -6.0, 6.0)
    return (values * amplitude[:, None, None]).astype(jnp.bfloat16)


def draw_counts(key, part):
    blocks = K // OWNED
    others = OWNED - 1
    rest = SLOTS - PMAX
    even = rest // others
    extra = rest % others
    index = jnp.arange(others, dtype=jnp.int32)
    base = even + (index < extra).astype(jnp.int32)
    half = others // 2
    first = base[0:2 * half:2]
    second = base[1:2 * half:2]
    limit = jnp.minimum(jnp.minimum(first - 1, PMAX - first), jnp.minimum(second - 1, PMAX - second))
    key_shift = jax.random.fold_in(key, 11)
    key_perm = jax.random.fold_in(key, 23)
    shift = jax.random.randint(key_shift, (blocks, half), -limit[None, :], limit[None, :] + 1)
    paired = jnp.stack([first[None, :] + shift, second[None, :] - shift], -1).reshape(blocks, 2 * half)
    tail = jnp.broadcast_to(base[2 * half:][None, :], (blocks, others - 2 * half))
    peak = jnp.full((blocks, 1), PMAX, dtype=jnp.int32)
    whole = jnp.concatenate([paired, tail, peak], 1).astype(jnp.int32)
    perms = jax.vmap(lambda single: jax.random.permutation(single, OWNED))(jax.random.split(key_perm, blocks))
    placed = jnp.take_along_axis(whole, perms.astype(jnp.int32), 1)
    return placed.reshape(K).astype(jnp.int32)


def with_ends(drawn, stream_key, low, largest):
    longest = drawn.shape.index(max(drawn.shape))
    spots = []
    for shift in (0, 1):
        where = [jax.random.randint(jax.random.fold_in(stream_key, axis), (), 0, length) for axis, length in enumerate(drawn.shape)]
        where[longest] = (where[longest] + shift) % drawn.shape[longest]
        spots.append(tuple(where))
    return drawn.at[spots[0]].set(low).at[spots[1]].set(largest)


def normal_values(stream_key, extent, scale, reach, kind=jnp.bfloat16):
    return jnp.clip(scale * jax.random.normal(stream_key, extent, jnp.float32), -reach, reach).astype(kind)


def setup_inputs(seed: int = 0) -> dict:
    arg_keys = jax.random.split(jax.random.key(seed), 7)
    images = draw_images(jax.random.fold_in(arg_keys[6], 71), 0)
    group_ids = with_ends(jax.random.randint(arg_keys[1], (IMAGES,), 0, G), jax.random.fold_in(arg_keys[1], 1), 0, G - 1).astype(jnp.int32)
    counts = draw_counts(jax.random.fold_in(arg_keys[6], 71), 0)
    radial_basis = normal_values(arg_keys[3], (K, R, PMAX), R ** -0.5, 0.5)
    ctf_gain = jnp.clip(jnp.exp(jax.random.uniform(arg_keys[4], (G, K), jnp.float32, math.log(0.2), math.log(2.0))), 0.2, 2.0)
    noise_var = jnp.clip(jnp.exp(jax.random.uniform(arg_keys[5], (K,), jnp.float32, math.log(0.25), math.log(2.0))), 0.25, 2.0)
    return dict(images=images, group_ids=group_ids, counts=counts, radial_basis=radial_basis, ctf_gain=ctf_gain, noise_var=noise_var)


def dft_tables(angles, freqs):
    angle_index = jnp.arange(angles, dtype=jnp.int32)
    freq_index = jnp.arange(freqs, dtype=jnp.int32)
    turns = angle_index[:, None] * freq_index[None, :] % angles
    phases = turns.astype(jnp.float32) * (2.0 * math.pi / angles)
    factor = 1.0 / math.sqrt(angles)
    cosine = jnp.cos(phases) * factor
    sine = -jnp.sin(phases) * factor
    forward = jnp.concatenate([cosine, sine], 1).astype(jnp.bfloat16)
    doubling = jnp.where(freq_index == 0, 1.0, 2.0).astype(jnp.float32)
    inverse = jnp.concatenate([cosine * doubling[None, :], sine * doubling[None, :]], 1).T.astype(jnp.bfloat16)
    return (forward, inverse)

def shrink_cov(gram, fourth, total, used, image_total):
    sample = gram / total[:, None, None]
    ident = used[:, :, None] * jnp.eye(used.shape[1], dtype=jnp.float32)[None]
    level = jnp.trace(sample, axis1=1, axis2=2) / lax.optimization_barrier(jnp.sum(used, 1))
    spread = lax.optimization_barrier(jnp.sum((sample - level[:, None, None] * ident) ** 2, (1, 2)))
    excess = (fourth / total - lax.optimization_barrier(jnp.sum(sample * sample, (1, 2)))) / (2.0 * image_total)
    weight = excess / (excess + spread)
    return (1.0 - weight)[:, None, None] * sample + (weight * level)[:, None, None] * ident

def wiener_filters(cov, gain, noise_level, steps_count):
    identity = jnp.eye(cov.shape[1], dtype=jnp.float32)[None]
    system = (gain * gain)[:, None, None] * cov + noise_level[:, None, None] * identity
    frobenius = jnp.sqrt(lax.optimization_barrier(jnp.sum(system * system, (1, 2))))
    approx = identity / frobenius[:, None, None]
    for sweep in range(steps_count):
        middle = jnp.matmul(approx, system, precision=lax.Precision.HIGHEST)
        approx = 2.0 * approx - jnp.matmul(middle, approx, precision=lax.Precision.HIGHEST)
    product = jnp.matmul(cov, approx, precision=lax.Precision.HIGHEST)
    return (gain[:, None, None] * product).astype(jnp.bfloat16)

def reference(images, group_ids, counts, radial_basis, ctf_gain, noise_var):
    forward, inverse = dft_tables(A, K)
    used = (jnp.arange(PMAX, dtype=jnp.int32)[None, :] < counts[:, None]).astype(jnp.float32)
    basis_used = (radial_basis.astype(jnp.float32) * used[:, None, :]).astype(jnp.bfloat16)
    spectrum = jnp.dot(images.reshape(IMAGES * R, A), forward, preferred_element_type=jnp.float32)
    spectrum = spectrum.astype(jnp.bfloat16).reshape(IMAGES, R, 2, K)
    coeffs = jnp.einsum('nrck,krp->kcnp', spectrum.astype(jnp.float32), basis_used.astype(jnp.float32)).astype(jnp.bfloat16)
    coeff_wide = coeffs.astype(jnp.float32)
    gains_kn = jnp.take(ctf_gain, group_ids, axis=0).T
    scaled = (coeff_wide * gains_kn[:, None, :, None]).astype(jnp.bfloat16).astype(jnp.float32)
    gram = jnp.einsum('kcnp,kcnq->kpq', scaled, scaled)
    norms = lax.optimization_barrier(jnp.sum(coeff_wide * coeff_wide, -1))
    squares = gains_kn * gains_kn
    fourth = lax.optimization_barrier(jnp.sum(squares[:, None, :] * norms * norms, (1, 2)))
    total = 2.0 * lax.optimization_barrier(jnp.sum(squares, 1))
    cov = shrink_cov(gram, fourth, total, used, IMAGES)
    cov_all = jnp.broadcast_to(cov[None], (G, K, PMAX, PMAX)).reshape(G * K, PMAX, PMAX)
    filters = wiener_filters(cov_all, ctf_gain.reshape(G * K), jnp.tile(noise_var, G), NS_ITERS)
    filters = filters.reshape(G, K, PMAX, PMAX).astype(jnp.float32)
    result = jnp.zeros((K, 2, IMAGES, PMAX), jnp.float32)
    for which_group in range(G):
        part = jnp.einsum('kcnq,kpq->kcnp', coeff_wide, filters[which_group])
        result = result + jnp.where((group_ids == which_group)[None, None, :, None], part, 0.0)
    cleaned = result.astype(jnp.bfloat16).astype(jnp.float32)
    back = jnp.einsum('kcnp,krp->nrck', cleaned, basis_used.astype(jnp.float32)).astype(jnp.bfloat16)
    back = back.reshape(IMAGES * R, 2 * K)
    denoised = jnp.dot(back, inverse, preferred_element_type=jnp.float32).astype(jnp.bfloat16)
    return denoised.reshape(IMAGES, R, A)
```

```python
import functools
import math

import jax
import jax.numpy as jnp
from jax import lax
from jax.experimental import pallas as pl
from jax.experimental.pallas import tpu as pltpu
from jax.sharding import PartitionSpec as P

NS_ITERS = 7
SIDE = 4
MESH_ID = pl.DeviceIdType.MESH
VMEM = pl.BlockSpec(memory_space=pltpu.VMEM)
SMEM = pl.BlockSpec(memory_space=pltpu.SMEM)
F32 = jnp.float32
BF16 = jnp.bfloat16


def place():
    img = lax.axis_index("img")
    grp = lax.axis_index("grp")
    return grp // 2, img // 8, img % 8, grp % 2


def owner_index(x, y, z):
    return x * 8 + y * 2 + z % 2


def hops(step):
    return min(step, SIDE - step)


def exchange_steps():
    steps = [(a, b, c) for a in range(SIDE) for b in range(SIDE) for c in range(2)]
    steps.remove((0, 0, 0))
    steps.sort(key=lambda s: -(hops(s[0]) + hops(s[1]) + s[2]))
    return steps


def exchange_kernel(with_ids, *refs):
    if with_ids:
        data, ids, out, ids_out, local, send, recv, local_ids, send_ids, recv_ids = refs
    else:
        data, out, local, send, recv = refs
    x, y, z, core = place()
    me = owner_index(x, y, z)
    steps = exchange_steps()
    peers = []
    for a, b, c in steps:
        px, py, pz = (x + a) % SIDE, (y + b) % SIDE, z // 2 * 2 + (z + c) % 2
        peers.append(({"img": py * 8 + pz, "grp": px * 2 + core}, owner_index(px, py, pz)))
    barrier = pltpu.get_barrier_semaphore()
    for device, _ in peers:
        pl.semaphore_signal(barrier, inc=1, device_id=device, device_id_type=MESH_ID)
    own = [pltpu.make_async_copy(data.at[me], out.at[me], local)]
    if with_ids:
        own.append(pltpu.make_async_copy(ids, ids_out.at[me], local_ids))
    for copy in own:
        copy.start()
    pl.semaphore_wait(barrier, len(peers))
    copies = []
    for i, (device, index) in enumerate(peers):
        copies.append(
            pltpu.make_async_remote_copy(
                data.at[index], out.at[me], send.at[i], recv.at[i],
                device_id=device, device_id_type=MESH_ID,
            )
        )
        if with_ids:
            copies.append(
                pltpu.make_async_remote_copy(
                    ids, ids_out.at[me], send_ids.at[i], recv_ids.at[i],
                    device_id=device, device_id_type=MESH_ID,
                )
            )
    for copy in copies:
        copy.start()
    for copy in own + copies:
        copy.wait()


def exchange(data, ids, collective_id):
    count = data.shape[0] - 1
    dma = pltpu.SemaphoreType.DMA
    scratch = [dma, dma((count,)), dma((count,))]
    operands, shapes = [data], [jax.ShapeDtypeStruct(data.shape, data.dtype)]
    if ids is not None:
        operands.append(ids)
        shapes.append(jax.ShapeDtypeStruct((data.shape[0], *ids.shape), ids.dtype))
        scratch = scratch * 2
    return pl.pallas_call(
        functools.partial(exchange_kernel, ids is not None),
        out_shape=shapes,
        in_specs=[VMEM] * len(operands),
        out_specs=[VMEM] * len(operands),
        scratch_shapes=scratch,
        compiler_params=pltpu.CompilerParams(collective_id=collective_id, has_side_effects=True),
        name="exchange",
    )(*operands)


def lanes(shape):
    return lax.broadcasted_iota(jnp.int32, shape, len(shape) - 1)


def tile(index):
    return pl.ds(pl.multiple_of(index * 128, 128), 128)


def block_slots(counts, first):
    offsets, offset = [], 0
    for j in range(4):
        count = counts[first + j]
        offsets.append((offset, count))
        offset = offset + count
    return offsets


def pack_kernel(counts, coeffs, out, wide):
    lane = lanes((64, 128))

    @pl.loop(0, 32)
    def _(block):
        wide[...] = jnp.zeros_like(wide)
        for j, (offset, count) in enumerate(block_slots(counts, block * 4)):
            value = jnp.where(lane < count, coeffs[block * 4 + j].astype(F32), 0.0)
            shift, first = offset % 128, offset // 128
            turned = pltpu.roll(value, shift, 1)
            wide[:, tile(first)] += jnp.where(lane >= shift, turned, 0.0)
            wide[:, tile(first + 1)] += jnp.where(lane < shift, turned, 0.0)
        fold_slots(wide[:, 0:128], wide[:, 128:256], wide[:, 256:384], out.at[block])


def fold_slots(low, middle, high, out):
    out[0:64] = low.astype(BF16)
    out[64:128] = middle.astype(BF16)
    lane = lanes((32, 128))
    out[128:160] = jnp.where(lane < 64, high[0:32], pltpu.roll(high[32:64], 64, 1)).astype(BF16)


def unfold_slots(high):
    lane = lanes((32, 128))
    high = high.astype(F32)
    first = jnp.where(lane < 64, high, 0.0)
    second = jnp.where(lane < 64, pltpu.roll(high, 64, 1), 0.0)
    return jnp.concatenate([first, second], 0)


def unpack_kernel(counts, packed, out, wide):
    lane = lanes((64, 128))
    wide[...] = jnp.zeros_like(wide)

    @pl.loop(0, 32)
    def _(block):
        wide[:, 0:128] = packed[block, 0:64].astype(F32)
        wide[:, 128:256] = packed[block, 64:128].astype(F32)
        wide[:, 256:384] = unfold_slots(packed[block, 128:160])
        for j, (offset, count) in enumerate(block_slots(counts, block * 4)):
            shift, first = offset % 128, offset // 128
            back = (128 - shift) % 128
            low = pltpu.roll(wide[:, tile(first)], back, 1)
            high = pltpu.roll(wide[:, tile(first + 1)], back, 1)
            value = jnp.where(lane < 128 - shift, low, high)
            out[block * 4 + j] = jnp.where(lane < count, value, 0.0).astype(BF16)


def chunk_slots(packed, start):
    rows = [packed[start + s] for s in range(4)]
    low = jnp.concatenate([r[0:64] for r in rows], 0).astype(F32)
    middle = jnp.concatenate([r[64:128] for r in rows], 0).astype(F32)
    high = jnp.concatenate([unfold_slots(r[128:160]) for r in rows], 0)
    return low, middle, high


def gram_kernel(counts, gains, packed, ids, out, gram, table, member):
    x, y, z, _ = place()
    first_freq = owner_index(x, y, z) * 4
    slots = block_slots(counts, first_freq)
    gram[...] = jnp.zeros_like(gram)
    row = lax.broadcasted_iota(jnp.int32, (8, 512), 0)
    lane = lanes((8, 512))
    slot_gain = jnp.zeros((8, 512), F32)
    for j, (offset, count) in enumerate(slots):
        column = jnp.zeros((8, 512), F32)
        for g in range(8):
            column = jnp.where(row == g, gains[g, first_freq + j], column)
        here = ((lane >= offset) & (lane < offset + count)) | (lane == 384 + j)
        slot_gain = jnp.where(here, column, slot_gain)
    high = slot_gain.astype(BF16).astype(F32)
    middle = (slot_gain - high).astype(BF16).astype(F32)
    low = slot_gain - high - middle
    table[...] = jnp.concatenate([high, middle, low, jnp.zeros((104, 512), F32)], 0).astype(BF16)
    row = lax.broadcasted_iota(jnp.int32, (384, 128), 0)
    lane = lanes((384, 128))
    inside = jnp.zeros((384, 128), F32)
    for j, (offset, count) in enumerate(slots):
        inside = jnp.where((lane == j) & (row >= offset) & (row < offset + count), 1.0, inside)
    member[...] = inside.astype(BF16)
    lane = lanes((256, 128))
    wanted = jnp.where(lane < 24, lane % 8, -1).astype(F32)

    def chunk(i, sums):
        fourth, total = sums
        value = jnp.concatenate(chunk_slots(packed, i * 4), 1)
        group = ids[pl.ds(pl.multiple_of(i * 256, 256), 256), :].astype(F32)
        onehot = jnp.where(group == wanted, 1.0, 0.0).astype(BF16)
        gain = jnp.dot(onehot, table[...], preferred_element_type=F32)
        scaled = (value * gain[:, 0:384]).astype(BF16)
        sums = lax.dot_general(
            scaled, scaled, (((0,), (0,)), ((), ())), preferred_element_type=F32
        )
        for t in range(3):
            gram[t, 0:384] += sums[:, t * 128 : t * 128 + 128]
        square = value * value
        upper = square.astype(BF16)
        lower = (square - upper.astype(F32)).astype(BF16)
        norms = jnp.dot(upper, member[...], preferred_element_type=F32)
        norms += jnp.dot(lower, member[...], preferred_element_type=F32)
        weight = gain[:, 384:512] * gain[:, 384:512]
        fourth += jnp.sum(weight * norms * norms, 0, keepdims=True)
        total += jnp.sum(weight, 0, keepdims=True)
        return fourth, total

    nothing = jnp.zeros((1, 128), F32)
    fourth, total = lax.fori_loop(0, 8, chunk, (nothing, nothing))
    row = lax.broadcasted_iota(jnp.int32, (128, 128), 0)
    lane = lanes((128, 128))
    for j, (offset, count) in enumerate(slots):
        shift, first = offset % 128, offset // 128
        back = (128 - shift) % 128
        low = pltpu.roll(gram[first, pl.ds(offset, 128)], back, 1)
        high = pltpu.roll(gram[first + 1, pl.ds(offset, 128)], back, 1)
        value = jnp.where(lane < 128 - shift, low, high)
        out[j, 0:128] = jnp.where((lane < count) & (row < count), value, 0.0)
        out[j, 128:136] = jnp.concatenate([fourth, total, jnp.zeros((6, 128), F32)], 0)


def reduce_kernel(part, out, other, mine, send, recv):
    x, y, z, core = place()
    quarter, low = z // 2, z % 2
    partner = {"img": y * 8 + z, "grp": x * 2 + 1 - core}
    column = []
    for step in (2, 1, 3):
        column.append({"img": y * 8 + (quarter + step) % 4 * 2 + low, "grp": x * 2 + core})
    barrier = pltpu.get_barrier_semaphore()
    for device in [partner] + column:
        pl.semaphore_signal(barrier, inc=1, device_id=device, device_id_type=MESH_ID)
    pl.semaphore_wait(barrier, 4)
    swap = pltpu.make_async_remote_copy(
        part.at[pl.ds((1 - core) * 2, 2)], other, send.at[0], recv.at[0],
        device_id=partner, device_id_type=MESH_ID,
    )
    swap.start()
    swap.wait()
    both = part[pl.ds(core * 2, 2)] + other[...]
    mine[...] = both
    copies = []
    for i, device in enumerate(column):
        copies.append(
            pltpu.make_async_remote_copy(
                mine, out.at[quarter], send.at[i + 1], recv.at[i + 1],
                device_id=device, device_id_type=MESH_ID,
            )
        )
    for copy in copies:
        copy.start()
    out[quarter] = both
    for copy in copies:
        copy.wait()


def split(value):
    high = value.astype(BF16)
    return high, (value - high.astype(F32)).astype(BF16)


def right_side(value):
    high, low = split(value)
    return jnp.concatenate(
        [jnp.concatenate([high, low], 1), jnp.concatenate([high, jnp.zeros_like(high)], 1)], 0
    )


def product(left, right):
    high, low = split(left)
    wide = jnp.dot(jnp.concatenate([high, low], 1), right, preferred_element_type=F32)
    return wide[:, 0:128] + wide[:, 128:256]


def total_of(value):
    return jnp.sum(jnp.sum(value, 0, keepdims=True), 1, keepdims=True)


def filter_kernel(images, counts, gains, noise, parts, out, cov_ref, cov_right, size, trace):
    x, y, z, core = place()
    first_freq = owner_index(x, y, z) * 4 + core * 2
    row = lax.broadcasted_iota(jnp.int32, (128, 128), 0)
    lane = lanes((128, 128))
    line = lanes((1, 128))
    for j in range(2):
        block = ((parts[0, j] + parts[1, j]) + parts[2, j]) + parts[3, j]
        count = counts[first_freq + j]
        here = line == core * 2 + j
        fourth = jnp.sum(jnp.where(here, block[128:129], 0.0), 1, keepdims=True)
        total = jnp.sum(jnp.where(here, block[129:130], 0.0), 1, keepdims=True)
        sample = block[0:128] / total
        ident = jnp.where((row == lane) & (row < count), 1.0, 0.0)
        level = total_of(sample * ident) / count.astype(F32)
        off_level = sample - level * ident
        spread = total_of(off_level * off_level)
        excess = (fourth / total - total_of(sample * sample)) / (2.0 * images)
        weight = excess / (excess + spread)
        cov = (1.0 - weight) * sample + (weight * level) * ident
        cov_ref[j] = cov
        cov_right[j] = right_side(cov)
        size[j] = jnp.broadcast_to(total_of(cov * cov), (8, 128))
        trace[j] = jnp.broadcast_to(total_of(cov * ident), (8, 128))
    ident = jnp.where(row == lane, 1.0, 0.0)

    @pl.loop(0, 4)
    def _(pair):
        problems = [(pair * 2 + g, j) for g in range(2) for j in range(2)]
        powers, sums, scales = [], [], []
        for g, j in problems:
            gain, level = gains[g, first_freq + j], noise[first_freq + j]
            square = gain * gain
            norm = size[j, 0:1, 0:1] * (square * square)
            norm += trace[j, 0:1, 0:1] * (2.0 * square * level) + 128.0 * level * level
            scale = 1.0 / jnp.sqrt(norm)
            power = (1.0 - scale * level) * ident - (scale * square) * cov_ref[j]
            powers.append(power)
            sums.append(ident + power)
            scales.append(scale * gain)
        powers = [product(p, right_side(p)) for p in powers]
        for _ in range(NS_ITERS - 2):
            sides = [right_side(p) for p in powers]
            both = [
                product(jnp.concatenate([s, p], 0), r) for s, p, r in zip(sums, powers, sides)
            ]
            sums = [s + b[0:128] for s, b in zip(sums, both)]
            powers = [b[128:256] for b in both]
        sums = [s + product(s, right_side(p)) for s, p in zip(sums, powers)]
        for (g, j), s, scale in zip(problems, sums, scales):
            out[j, g] = (scale * product(s, cov_right[j])).astype(BF16)


def swap_kernel(mine, out, send, recv):
    x, y, z, core = place()
    partner = {"img": y * 8 + z, "grp": x * 2 + 1 - core}
    barrier = pltpu.get_barrier_semaphore()
    pl.semaphore_signal(barrier, inc=1, device_id=partner, device_id_type=MESH_ID)
    pl.semaphore_wait(barrier, 1)
    copy = pltpu.make_async_remote_copy(
        mine, out, send, recv, device_id=partner, device_id_type=MESH_ID
    )
    copy.start()
    copy.wait()


def apply_kernel(counts, packed, ids, mine, other, out, wide, filters):
    x, y, z, core = place()
    first_freq = owner_index(x, y, z) * 4
    slots = block_slots(counts, first_freq)
    lane = lanes((128, 128))

    @pl.loop(0, 8)
    def _(g):
        wide[...] = jnp.zeros_like(wide)
        for j, (offset, _) in enumerate(slots):
            value = jnp.where(core == j // 2, mine[j % 2, g].astype(F32), other[j % 2, g].astype(F32))
            shift, first = offset % 128, offset // 128
            turned = pltpu.roll(value, shift, 1)
            wide[first, pl.ds(offset, 128)] += jnp.where(lane >= shift, turned, 0.0)
            wide[first + 1, pl.ds(offset, 128)] += jnp.where(lane < shift, turned, 0.0)
        row = pl.ds(pl.multiple_of(g * 384, 384), 384)
        for t in range(3):
            filters[row, t * 128 : t * 128 + 128] = wide[t, 0:384].astype(BF16)

    @pl.loop(0, 8)
    def _(i):
        value = jnp.concatenate(chunk_slots(packed, i * 4), 1).astype(BF16)
        group = ids[pl.ds(pl.multiple_of(i * 256, 256), 256), :].astype(F32)
        pieces = []
        for g in range(8):
            mask = jnp.where(group == float(g), 1.0, 0.0).astype(BF16)
            pieces.append(value * jnp.concatenate([mask] * 3, 1))
        cleaned = jnp.dot(jnp.concatenate(pieces, 1), filters[...], preferred_element_type=F32)
        for s in range(4):
            rows = cleaned[s * 64 : s * 64 + 64]
            fold_slots(rows[:, 0:128], rows[:, 128:256], rows[:, 256:384], out.at[i * 4 + s])


def local_call(kernel, shape, dtype, in_specs, scratch, name, *operands):
    return pl.pallas_call(
        kernel,
        out_shape=jax.ShapeDtypeStruct(shape, dtype),
        in_specs=in_specs,
        out_specs=VMEM,
        scratch_shapes=scratch,
        name=name,
    )(*operands)


def remote_call(kernel, shape, dtype, scratch, collective_id, name, operand):
    return pl.pallas_call(
        kernel,
        out_shape=jax.ShapeDtypeStruct(shape, dtype),
        in_specs=[VMEM],
        out_specs=VMEM,
        scratch_shapes=scratch,
        compiler_params=pltpu.CompilerParams(collective_id=collective_id, has_side_effects=True),
        name=name,
    )(operand)


def dft_tables(angles, freqs):
    angle_index = jnp.arange(angles, dtype=jnp.int32)
    freq_index = jnp.arange(freqs, dtype=jnp.int32)
    turns = angle_index[:, None] * freq_index[None, :] % angles
    phases = turns.astype(jnp.float32) * (2.0 * math.pi / angles)
    factor = 1.0 / math.sqrt(angles)
    cosine = jnp.cos(phases) * factor
    sine = -jnp.sin(phases) * factor
    forward = jnp.concatenate([cosine, sine], 1).astype(jnp.bfloat16)
    doubling = jnp.where(freq_index == 0, 1.0, 2.0).astype(jnp.float32)
    inverse = jnp.concatenate([cosine * doubling[None, :], sine * doubling[None, :]], 1).T.astype(
        jnp.bfloat16
    )
    return (forward, inverse)


def body(images, group_ids, counts, radial_basis, ctf_gain, noise_var):
    local_images, radii, angles = images.shape
    freqs = radial_basis.shape[0]
    image_total = local_images * lax.axis_size("img") * lax.axis_size("grp")
    dma = pltpu.SemaphoreType.DMA
    forward, inverse = dft_tables(angles, freqs)
    spectrum = jnp.dot(
        images.reshape(local_images * radii, angles), forward, preferred_element_type=F32
    )
    spectrum = spectrum.astype(BF16).reshape(local_images, radii, 2, freqs)
    coeffs = jnp.einsum(
        "nrck,krp->kcnp", spectrum, radial_basis, preferred_element_type=F32
    ).astype(BF16).reshape(freqs, 64, 128)
    packed = local_call(
        pack_kernel, (32, 160, 128), BF16, [SMEM, VMEM], [pltpu.VMEM((64, 512), F32)],
        "pack", counts, coeffs,
    )
    ids = jnp.pad(group_ids, (0, 96)).reshape(1, 128)
    arrived, all_ids = exchange(packed, ids, 0)
    row_ids = jnp.broadcast_to(
        all_ids[:, 0, None, 0:32, None], (32, 2, 32, 128)
    ).astype(BF16).reshape(2048, 128)
    gram = local_call(
        gram_kernel, (4, 136, 128), F32, [SMEM, SMEM, VMEM, VMEM],
        [pltpu.VMEM((4, 512, 128), F32), pltpu.VMEM((128, 512), BF16), pltpu.VMEM((384, 128), BF16)],
        "gram", counts, ctf_gain, arrived, row_ids,
    )
    parts = remote_call(
        reduce_kernel, (4, 2, 136, 128), F32,
        [pltpu.VMEM((2, 136, 128), F32), pltpu.VMEM((2, 136, 128), F32), dma((4,)), dma((4,))],
        1, "reduce", gram,
    )
    filters = local_call(
        functools.partial(filter_kernel, image_total), (2, 8, 128, 128), BF16,
        [SMEM, SMEM, SMEM, VMEM],
        [
            pltpu.VMEM((2, 128, 128), F32), pltpu.VMEM((2, 256, 256), BF16),
            pltpu.VMEM((2, 8, 128), F32), pltpu.VMEM((2, 8, 128), F32),
        ],
        "filters", counts, ctf_gain, noise_var, parts,
    )
    partner = remote_call(swap_kernel, filters.shape, BF16, [dma, dma], 2, "swap", filters)
    cleaned = local_call(
        apply_kernel, (32, 160, 128), BF16, [SMEM, VMEM, VMEM, VMEM, VMEM],
        [pltpu.VMEM((4, 512, 128), F32), pltpu.VMEM((3072, 384), BF16)],
        "apply", counts, arrived, row_ids, filters, partner,
    )
    (returned,) = exchange(cleaned, None, 3)
    spread = local_call(
        unpack_kernel, (freqs, 64, 128), BF16, [SMEM, VMEM], [pltpu.VMEM((64, 512), F32)],
        "unpack", counts, returned,
    ).reshape(freqs, 2, local_images, 128)
    back = jnp.einsum(
        "kcnp,krp->nrck", spread, radial_basis, preferred_element_type=F32
    ).astype(BF16)
    back = back.reshape(local_images * radii, 2 * freqs)
    denoised = jnp.dot(back, inverse, preferred_element_type=F32).astype(BF16)
    return denoised.reshape(local_images, radii, angles)


def solution(mesh):
    placed = (P(("img", "grp"), None, None), P(("img", "grp")), P(), P(), P(), P())
    return jax.shard_map(
        body, mesh=mesh, in_specs=placed, out_specs=P(("img", "grp"), None, None), check_vma=False
    )
```

```python
import functools
import math

import jax
import jax.numpy as jnp
from jax import lax
from jax.experimental import pallas as pl
from jax.experimental.pallas import tpu as pltpu
from jax.sharding import PartitionSpec as P

NS_ITERS = 7
SIDE = 4
MESH_ID = pl.DeviceIdType.MESH
VMEM = pl.BlockSpec(memory_space=pltpu.VMEM)
SMEM = pl.BlockSpec(memory_space=pltpu.SMEM)
F32 = jnp.float32
BF16 = jnp.bfloat16


def place():
    img = lax.axis_index("img")
    grp = lax.axis_index("grp")
    return grp // 2, img // 8, img % 8, grp % 2


def owner_index(x, y, z):
    return x * 8 + y * 2 + z % 2


def hops(step):
    return min(step, SIDE - step)


def exchange_steps():
    steps = [(a, b, c) for a in range(SIDE) for b in range(SIDE) for c in range(2)]
    steps.remove((0, 0, 0))
    steps.sort(key=lambda s: -(hops(s[0]) + hops(s[1]) + s[2]))
    return steps


def exchange_kernel(with_ids, *refs):
    if with_ids:
        data, ids, out, ids_out, local, send, recv, local_ids, send_ids, recv_ids = refs
    else:
        data, out, local, send, recv = refs
    x, y, z, core = place()
    me = owner_index(x, y, z)
    steps = exchange_steps()
    peers = []
    for a, b, c in steps:
        px, py, pz = (x + a) % SIDE, (y + b) % SIDE, z // 2 * 2 + (z + c) % 2
        peers.append(({"img": py * 8 + pz, "grp": px * 2 + core}, owner_index(px, py, pz)))
    barrier = pltpu.get_barrier_semaphore()
    for device, _ in peers:
        pl.semaphore_signal(barrier, inc=1, device_id=device, device_id_type=MESH_ID)
    own = [pltpu.make_async_copy(data.at[me], out.at[me], local)]
    if with_ids:
        own.append(pltpu.make_async_copy(ids, ids_out.at[me], local_ids))
    for copy in own:
        copy.start()
    pl.semaphore_wait(barrier, len(peers))
    copies = []
    for i, (device, index) in enumerate(peers):
        copies.append(
            pltpu.make_async_remote_copy(
                data.at[index], out.at[me], send.at[i], recv.at[i],
                device_id=device, device_id_type=MESH_ID,
            )
        )
        if with_ids:
            copies.append(
                pltpu.make_async_remote_copy(
                    ids, ids_out.at[me], send_ids.at[i], recv_ids.at[i],
                    device_id=device, device_id_type=MESH_ID,
                )
            )
    for copy in copies:
        copy.start()
    for copy in own + copies:
        copy.wait()


def exchange(data, ids, collective_id):
    count = data.shape[0] - 1
    dma = pltpu.SemaphoreType.DMA
    scratch = [dma, dma((count,)), dma((count,))]
    operands, shapes = [data], [jax.ShapeDtypeStruct(data.shape, data.dtype)]
    if ids is not None:
        operands.append(ids)
        shapes.append(jax.ShapeDtypeStruct((data.shape[0], *ids.shape), ids.dtype))
        scratch = scratch * 2
    return pl.pallas_call(
        functools.partial(exchange_kernel, ids is not None),
        out_shape=shapes,
        in_specs=[VMEM] * len(operands),
        out_specs=[VMEM] * len(operands),
        scratch_shapes=scratch,
        compiler_params=pltpu.CompilerParams(collective_id=collective_id, has_side_effects=True),
        name="exchange",
    )(*operands)


def lanes(shape):
    return lax.broadcasted_iota(jnp.int32, shape, len(shape) - 1)


def tile(index):
    return pl.ds(pl.multiple_of(index * 128, 128), 128)


def block_slots(counts, first):
    offsets, offset = [], 0
    for j in range(4):
        count = counts[first + j]
        offsets.append((offset, count))
        offset = offset + count
    return offsets


def slot_mask(lane, t, offset, count):
    slot = lane + t * 128
    return (slot >= offset) & (slot < offset + count)


def pack_block(counts, coeffs, block, out):
    lane = lanes((64, 128))
    tiles = [jnp.zeros((64, 128), F32) for _ in range(3)]
    for j, (offset, count) in enumerate(block_slots(counts, block * 4)):
        turned = pltpu.roll(coeffs[block * 4 + j].astype(F32), offset % 128, 1)
        tiles = [
            jnp.where(slot_mask(lane, t, offset, count), turned, tiles[t]) for t in range(3)
        ]
    fold_slots(*tiles, out.at[block])


def pack_kernel(counts, coeffs, out):
    @pl.loop(0, 16)
    def _(pair):
        for half in range(2):
            pack_block(counts, coeffs, pair * 2 + half, out)


def fold_slots(low, middle, high, out):
    out[0:64] = low.astype(BF16)
    out[64:128] = middle.astype(BF16)
    lane = lanes((32, 128))
    out[128:160] = jnp.where(lane < 64, high[0:32], pltpu.roll(high[32:64], 64, 1)).astype(BF16)


def unfold_slots(high):
    lane = lanes((32, 128))
    high = high.astype(F32)
    first = jnp.where(lane < 64, high, 0.0)
    second = jnp.where(lane < 64, pltpu.roll(high, 64, 1), 0.0)
    return jnp.concatenate([first, second], 0)


def pick_slots(tiles, lane, offset, count):
    picked = jnp.zeros_like(tiles[0])
    for t in range(3):
        picked = jnp.where(slot_mask(lane, t, offset, count), tiles[t], picked)
    return pltpu.roll(picked, (128 - offset % 128) % 128, 1)


def unpack_kernel(counts, packed, out):
    lane = lanes((64, 128))

    @pl.loop(0, 16)
    def _(pair):
        for half in range(2):
            block = pair * 2 + half
            tiles = [
                packed[block, 0:64].astype(F32),
                packed[block, 64:128].astype(F32),
                unfold_slots(packed[block, 128:160]),
            ]
            for j, (offset, count) in enumerate(block_slots(counts, block * 4)):
                out[block * 4 + j] = pick_slots(tiles, lane, offset, count).astype(BF16)


def chunk_slots(packed, start):
    rows = [packed[start + s] for s in range(4)]
    low = jnp.concatenate([r[0:64] for r in rows], 0).astype(F32)
    middle = jnp.concatenate([r[64:128] for r in rows], 0).astype(F32)
    high = jnp.concatenate([unfold_slots(r[128:160]) for r in rows], 0)
    return low, middle, high


def gram_kernel(counts, gains, packed, ids, out, gram, table, member):
    x, y, z, _ = place()
    first_freq = owner_index(x, y, z) * 4
    slots = block_slots(counts, first_freq)
    gram[...] = jnp.zeros_like(gram)
    row = lax.broadcasted_iota(jnp.int32, (8, 512), 0)
    lane = lanes((8, 512))
    slot_gain = jnp.zeros((8, 512), F32)
    for j, (offset, count) in enumerate(slots):
        column = jnp.zeros((8, 512), F32)
        for g in range(8):
            column = jnp.where(row == g, gains[g, first_freq + j], column)
        here = ((lane >= offset) & (lane < offset + count)) | (lane == 384 + j)
        slot_gain = jnp.where(here, column, slot_gain)
    high = slot_gain.astype(BF16).astype(F32)
    middle = (slot_gain - high).astype(BF16).astype(F32)
    low = slot_gain - high - middle
    table[...] = jnp.concatenate([high, middle, low, jnp.zeros((104, 512), F32)], 0).astype(BF16)
    row = lax.broadcasted_iota(jnp.int32, (384, 128), 0)
    lane = lanes((384, 128))
    inside = jnp.zeros((384, 128), F32)
    for j, (offset, count) in enumerate(slots):
        inside = jnp.where((lane == j) & (row >= offset) & (row < offset + count), 1.0, inside)
    member[...] = inside.astype(BF16)
    lane = lanes((256, 128))
    wanted = jnp.where(lane < 24, lane % 8, -1).astype(F32)

    def chunk(i, sums):
        fourth, total = sums
        value = jnp.concatenate(chunk_slots(packed, i * 4), 1)
        group = ids[pl.ds(pl.multiple_of(i * 256, 256), 256), :].astype(F32)
        onehot = jnp.where(group == wanted, 1.0, 0.0).astype(BF16)
        gain = jnp.dot(onehot, table[...], preferred_element_type=F32)
        scaled = (value * gain[:, 0:384]).astype(BF16)
        sums = lax.dot_general(
            scaled, scaled, (((0,), (0,)), ((), ())), preferred_element_type=F32
        )
        for t in range(3):
            gram[t, 0:384] += sums[:, t * 128 : t * 128 + 128]
        square = value * value
        upper = square.astype(BF16)
        lower = (square - upper.astype(F32)).astype(BF16)
        norms = jnp.dot(upper, member[...], preferred_element_type=F32)
        norms += jnp.dot(lower, member[...], preferred_element_type=F32)
        weight = gain[:, 384:512] * gain[:, 384:512]
        fourth += jnp.sum(weight * norms * norms, 0, keepdims=True)
        total += jnp.sum(weight, 0, keepdims=True)
        return fourth, total

    nothing = jnp.zeros((1, 128), F32)
    fourth, total = lax.fori_loop(0, 8, chunk, (nothing, nothing))
    row = lax.broadcasted_iota(jnp.int32, (128, 128), 0)
    lane = lanes((128, 128))
    squares = []
    for offset, count in slots:
        tiles = [gram[t, pl.ds(offset, 128)] for t in range(3)]
        squares.append(jnp.where(row < count, pick_slots(tiles, lane, offset, count), 0.0))
    for half in range(2):
        upper, lower = squares[half * 2], squares[half * 2 + 1]
        out[half, 0:128] = jnp.where(row <= lane, upper, lower)
        diagonal = jnp.sum(jnp.where(row == lane, lower, 0.0), 0, keepdims=True)
        out[half, 128:136] = jnp.concatenate(
            [diagonal, fourth, total, jnp.zeros((5, 128), F32)], 0
        )


def split(value):
    high = value.astype(BF16)
    return high, (value - high.astype(F32)).astype(BF16)


def right_side(value):
    high, low = split(value)
    return jnp.concatenate(
        [jnp.concatenate([high, low], 1), jnp.concatenate([high, jnp.zeros_like(high)], 1)], 0
    )


def product(left, right):
    high, low = split(left)
    wide = jnp.dot(jnp.concatenate([high, low], 1), right, preferred_element_type=F32)
    return wide[:, 0:128] + wide[:, 128:256]


def total_of(value):
    return jnp.sum(jnp.sum(value, 0, keepdims=True), 1, keepdims=True)


def middle_kernel(
    images, counts, gains, noise, part, out, out_other,
    other, mine, parts, cov_ref, cov_right, size, trace, send, recv,
):
    x, y, z, core = place()
    quarter, low = z // 2, z % 2
    partner = {"img": y * 8 + z, "grp": x * 2 + 1 - core}
    column = []
    for step in (2, 1, 3):
        column.append({"img": y * 8 + (quarter + step) % 4 * 2 + low, "grp": x * 2 + core})
    barrier = pltpu.get_barrier_semaphore()
    for device in [partner] + column:
        pl.semaphore_signal(barrier, inc=1, device_id=device, device_id_type=MESH_ID)
    pl.semaphore_wait(barrier, 4)

    def copy_to(source, target, index, device):
        return pltpu.make_async_remote_copy(
            source, target, send.at[index], recv.at[index],
            device_id=device, device_id_type=MESH_ID,
        )

    swap = copy_to(part.at[1 - core], other, 0, partner)
    swap.start()
    swap.wait()
    both = part[core] + other[...]
    mine[...] = both
    copies = [copy_to(mine, parts.at[quarter], i + 1, d) for i, d in enumerate(column)]
    for copy in copies:
        copy.start()
    parts[quarter] = both
    for copy in copies:
        copy.wait()
    make_covariances(images, counts, parts, cov_ref, cov_right, size, trace)

    def send_pair(pair):
        groups = pl.ds(pair * 2, 2)
        return copy_to(out.at[groups], out_other.at[groups], pair + 4, partner)

    @pl.loop(0, 4)
    def _(pair):
        make_filters(pair, gains, noise, out, cov_ref, cov_right, size, trace)
        send_pair(pair).start()

    for pair in range(4):
        send_pair(pair).wait()


def make_covariances(images, counts, parts, cov_ref, cov_right, size, trace):
    x, y, z, core = place()
    first_freq = owner_index(x, y, z) * 4 + core * 2
    row = lax.broadcasted_iota(jnp.int32, (128, 128), 0)
    lane = lanes((128, 128))
    line = lanes((1, 128))
    block = ((parts[0] + parts[1]) + parts[2]) + parts[3]
    square = block[0:128]
    above = jnp.where(row < lane, square, 0.0)
    below = jnp.where(row > lane, square, 0.0)
    grams = (
        jnp.where(row <= lane, square, 0.0) + above.T,
        jnp.where(row == lane, block[128:129], below) + below.T,
    )
    for j in range(2):
        count = counts[first_freq + j]
        here = line == core * 2 + j
        fourth = jnp.sum(jnp.where(here, block[129:130], 0.0), 1, keepdims=True)
        total = jnp.sum(jnp.where(here, block[130:131], 0.0), 1, keepdims=True)
        sample = grams[j] / total
        ident = jnp.where((row == lane) & (row < count), 1.0, 0.0)
        level = total_of(sample * ident) / count.astype(F32)
        off_level = sample - level * ident
        spread = total_of(off_level * off_level)
        excess = (fourth / total - total_of(sample * sample)) / (2.0 * images)
        weight = excess / (excess + spread)
        cov = (1.0 - weight) * sample + (weight * level) * ident
        cov_ref[j] = cov
        cov_right[j] = right_side(cov)
        size[j] = jnp.broadcast_to(total_of(cov * cov), (8, 128))
        trace[j] = jnp.broadcast_to(total_of(cov * ident), (8, 128))


def make_filters(pair, gains, noise, out, cov_ref, cov_right, size, trace):
    x, y, z, core = place()
    first_freq = owner_index(x, y, z) * 4 + core * 2
    ident = jnp.where(
        lax.broadcasted_iota(jnp.int32, (128, 128), 0) == lanes((128, 128)), 1.0, 0.0
    )
    problems = [(pair * 2 + g, j) for g in range(2) for j in range(2)]
    powers, sums, scales = [], [], []
    for g, j in problems:
        gain, level = gains[g, first_freq + j], noise[first_freq + j]
        square = gain * gain
        norm = size[j, 0:1, 0:1] * (square * square)
        norm += trace[j, 0:1, 0:1] * (2.0 * square * level) + 128.0 * level * level
        scale = 1.0 / jnp.sqrt(norm)
        power = (1.0 - scale * level) * ident - (scale * square) * cov_ref[j]
        powers.append(power)
        sums.append(ident + power)
        scales.append(scale * gain)
    powers = [product(p, right_side(p)) for p in powers]
    for _ in range(NS_ITERS - 2):
        sides = [right_side(p) for p in powers]
        both = [product(jnp.concatenate([s, p], 0), r) for s, p, r in zip(sums, powers, sides)]
        sums = [s + b[0:128] for s, b in zip(sums, both)]
        powers = [b[128:256] for b in both]
    sums = [s + product(s, right_side(p)) for s, p in zip(sums, powers)]
    for (g, j), s, scale in zip(problems, sums, scales):
        out[g, j] = (scale * product(s, cov_right[j])).astype(BF16)


def apply_kernel(counts, packed, ids, mine, other, out, wide, filters):
    x, y, z, core = place()
    first_freq = owner_index(x, y, z) * 4
    slots = block_slots(counts, first_freq)
    lane = lanes((128, 128))
    wide[...] = jnp.zeros_like(wide)

    @pl.loop(0, 8)
    def _(g):
        for j, (offset, count) in enumerate(slots):
            value = jnp.where(core == j // 2, mine[g, j % 2].astype(F32), other[g, j % 2].astype(F32))
            turned = pltpu.roll(value, offset % 128, 1)
            for t in range(3):
                wide[t, pl.ds(offset, 128)] = jnp.where(
                    slot_mask(lane, t, offset, count), turned, 0.0
                )
        row = pl.ds(pl.multiple_of(g * 384, 384), 384)
        for t in range(3):
            filters[row, t * 128 : t * 128 + 128] = wide[t, 0:384].astype(BF16)

    @pl.loop(0, 8)
    def _(i):
        value = jnp.concatenate(chunk_slots(packed, i * 4), 1).astype(BF16)
        group = ids[pl.ds(pl.multiple_of(i * 256, 256), 256), :].astype(F32)
        pieces = []
        for g in range(8):
            mask = jnp.where(group == float(g), 1.0, 0.0).astype(BF16)
            pieces.append(value * jnp.concatenate([mask] * 3, 1))
        cleaned = jnp.dot(jnp.concatenate(pieces, 1), filters[...], preferred_element_type=F32)
        for s in range(4):
            rows = cleaned[s * 64 : s * 64 + 64]
            fold_slots(rows[:, 0:128], rows[:, 128:256], rows[:, 256:384], out.at[i * 4 + s])


def local_call(kernel, shape, dtype, in_specs, scratch, name, *operands):
    return pl.pallas_call(
        kernel,
        out_shape=jax.ShapeDtypeStruct(shape, dtype),
        in_specs=in_specs,
        out_specs=VMEM,
        scratch_shapes=scratch,
        name=name,
    )(*operands)


def dft_tables(angles, freqs):
    angle_index = jnp.arange(angles, dtype=jnp.int32)
    freq_index = jnp.arange(freqs, dtype=jnp.int32)
    turns = angle_index[:, None] * freq_index[None, :] % angles
    phases = turns.astype(jnp.float32) * (2.0 * math.pi / angles)
    factor = 1.0 / math.sqrt(angles)
    cosine = jnp.cos(phases) * factor
    sine = -jnp.sin(phases) * factor
    forward = jnp.concatenate([cosine, sine], 1).astype(jnp.bfloat16)
    doubling = jnp.where(freq_index == 0, 1.0, 2.0).astype(jnp.float32)
    inverse = jnp.concatenate([cosine * doubling[None, :], sine * doubling[None, :]], 1).T.astype(
        jnp.bfloat16
    )
    return (forward, inverse)


def body(images, group_ids, counts, radial_basis, ctf_gain, noise_var):
    local_images, radii, angles = images.shape
    freqs = radial_basis.shape[0]
    image_total = local_images * lax.axis_size("img") * lax.axis_size("grp")
    dma = pltpu.SemaphoreType.DMA
    forward, inverse = dft_tables(angles, freqs)
    spectrum = jnp.dot(
        images.reshape(local_images * radii, angles), forward, preferred_element_type=F32
    )
    spectrum = spectrum.astype(BF16).reshape(local_images, radii, 2, freqs)
    coeffs = jnp.einsum(
        "nrck,krp->kcnp", spectrum, radial_basis, preferred_element_type=F32
    ).astype(BF16).reshape(freqs, 64, 128)
    packed = local_call(
        pack_kernel, (32, 160, 128), BF16, [SMEM, VMEM], [], "pack", counts, coeffs,
    )
    ids = jnp.pad(group_ids, (0, 96)).reshape(1, 128)
    arrived, all_ids = exchange(packed, ids, 0)
    row_ids = jnp.broadcast_to(
        all_ids[:, 0, None, 0:32, None], (32, 2, 32, 128)
    ).astype(BF16).reshape(2048, 128)
    gram = local_call(
        gram_kernel, (2, 136, 128), F32, [SMEM, SMEM, VMEM, VMEM],
        [pltpu.VMEM((3, 512, 128), F32), pltpu.VMEM((128, 512), BF16), pltpu.VMEM((384, 128), BF16)],
        "gram", counts, ctf_gain, arrived, row_ids,
    )
    filters = jax.ShapeDtypeStruct((8, 2, 128, 128), BF16)
    filters, partner = pl.pallas_call(
        functools.partial(middle_kernel, image_total),
        out_shape=[filters, filters],
        in_specs=[SMEM, SMEM, SMEM, VMEM],
        out_specs=[VMEM, VMEM],
        scratch_shapes=[
            pltpu.VMEM((136, 128), F32), pltpu.VMEM((136, 128), F32),
            pltpu.VMEM((4, 136, 128), F32),
            pltpu.VMEM((2, 128, 128), F32), pltpu.VMEM((2, 256, 256), BF16),
            pltpu.VMEM((2, 8, 128), F32), pltpu.VMEM((2, 8, 128), F32), dma((8,)), dma((8,)),
        ],
        compiler_params=pltpu.CompilerParams(collective_id=1, has_side_effects=True),
        name="middle",
    )(counts, ctf_gain, noise_var, gram)
    cleaned = local_call(
        apply_kernel, (32, 160, 128), BF16, [SMEM, VMEM, VMEM, VMEM, VMEM],
        [pltpu.VMEM((3, 512, 128), F32), pltpu.VMEM((3072, 384), BF16)],
        "apply", counts, arrived, row_ids, filters, partner,
    )
    (returned,) = exchange(cleaned, None, 2)
    spread = local_call(
        unpack_kernel, (freqs, 64, 128), BF16, [SMEM, VMEM], [], "unpack", counts, returned,
    ).reshape(freqs, 2, local_images, 128)
    back = jnp.einsum(
        "kcnp,krp->nrck", spread, radial_basis, preferred_element_type=F32
    ).astype(BF16)
    back = back.reshape(local_images * radii, 2 * freqs)
    denoised = jnp.dot(back, inverse, preferred_element_type=F32).astype(BF16)
    return denoised.reshape(local_images, radii, angles)


def solution(mesh):
    placed = (P(("img", "grp"), None, None), P(("img", "grp")), P(), P(), P(), P())
    return jax.shard_map(
        body, mesh=mesh, in_specs=placed, out_specs=P(("img", "grp"), None, None), check_vma=False
    )
```

```python
import functools
import math

import jax
import jax.numpy as jnp
from jax import lax
from jax.experimental import pallas as pl
from jax.experimental.pallas import tpu as pltpu
from jax.sharding import PartitionSpec as P

NS_ITERS = 7
SIDE = 4
MESH_ID = pl.DeviceIdType.MESH
VMEM = pl.BlockSpec(memory_space=pltpu.VMEM)
SMEM = pl.BlockSpec(memory_space=pltpu.SMEM)
F32 = jnp.float32
BF16 = jnp.bfloat16


def place():
    img = lax.axis_index("img")
    grp = lax.axis_index("grp")
    return grp // 2, img // 8, img % 8, grp % 2


def owner_index(x, y, z):
    return x * 8 + y * 2 + z % 2


def step_of(i):
    turn = i % 4
    return (turn + 1) % 4, (i // 4 + turn + 2) % 4, 1 - i // 16


def peer_of(i, sign):
    x, y, z, core = place()
    a, b, c = step_of(i)
    px, py = (x + SIDE + sign * a) % SIDE, (y + SIDE + sign * b) % SIDE
    pz = z // 2 * 2 + (z + c) % 2
    return {"img": py * 8 + pz, "grp": px * 2 + core}, owner_index(px, py, pz)


def lanes(shape):
    return lax.broadcasted_iota(jnp.int32, shape, len(shape) - 1)


def tile(index):
    return pl.ds(pl.multiple_of(index * 128, 128), 128)


def block_slots(counts, first):
    offsets, offset = [], 0
    for j in range(4):
        count = counts[first + j]
        offsets.append((offset, count))
        offset = offset + count
    return offsets


def slot_mask(lane, t, offset, count):
    slot = lane + t * 128
    return (slot >= offset) & (slot < offset + count)


def pack_block(counts, coeffs, block, out):
    lane = lanes((64, 128))
    tiles = [jnp.zeros((64, 128), F32) for _ in range(3)]
    for j, (offset, count) in enumerate(block_slots(counts, block * 4)):
        turned = pltpu.roll(coeffs[block * 4 + j].astype(F32), offset % 128, 1)
        tiles = [
            jnp.where(slot_mask(lane, t, offset, count), turned, tiles[t]) for t in range(3)
        ]
    fold_slots(*tiles, out.at[block])


def fold_slots(low, middle, high, out):
    out[0:64] = low.astype(BF16)
    out[64:128] = middle.astype(BF16)
    lane = lanes((32, 128))
    out[128:160] = jnp.where(lane < 64, high[0:32], pltpu.roll(high[32:64], 64, 1)).astype(BF16)


def unfold_slots(high):
    lane = lanes((32, 128))
    high = high.astype(F32)
    first = jnp.where(lane < 64, high, 0.0)
    second = jnp.where(lane < 64, pltpu.roll(high, 64, 1), 0.0)
    return jnp.concatenate([first, second], 0)


def pick_slots(tiles, lane, offset, count):
    picked = jnp.zeros_like(tiles[0])
    for t in range(3):
        picked = jnp.where(slot_mask(lane, t, offset, count), tiles[t], picked)
    return pltpu.roll(picked, (128 - offset % 128) % 128, 1)


def unpack_block(counts, packed, block, out):
    lane = lanes((64, 128))
    tiles = [
        packed[block, 0:64].astype(F32),
        packed[block, 64:128].astype(F32),
        unfold_slots(packed[block, 128:160]),
    ]
    for j, (offset, count) in enumerate(block_slots(counts, block * 4)):
        out[block * 4 + j] = pick_slots(tiles, lane, offset, count).astype(BF16)


def chunk_slots(packed, sources):
    rows = [packed[s] for s in sources]
    low = jnp.concatenate([r[0:64] for r in rows], 0).astype(F32)
    middle = jnp.concatenate([r[64:128] for r in rows], 0).astype(F32)
    high = jnp.concatenate([unfold_slots(r[128:160]) for r in rows], 0)
    return low, middle, high


def chunk_groups(ids, sources):
    rows = []
    for s in sources:
        column = pltpu.roll(ids[...], (128 - s) % 128, 1)[:, 0:1]
        rows += [jnp.broadcast_to(column, (32, 128))] * 2
    return jnp.concatenate(rows, 0)


def make_tables(slots, gains, first_freq, gram, table, member):
    gram[...] = jnp.zeros_like(gram)
    row = lax.broadcasted_iota(jnp.int32, (8, 512), 0)
    lane = lanes((8, 512))
    slot_gain = jnp.zeros((8, 512), F32)
    for j, (offset, count) in enumerate(slots):
        column = jnp.zeros((8, 512), F32)
        for g in range(8):
            column = jnp.where(row == g, gains[g, first_freq + j], column)
        here = ((lane >= offset) & (lane < offset + count)) | (lane == 384 + j)
        slot_gain = jnp.where(here, column, slot_gain)
    high = slot_gain.astype(BF16).astype(F32)
    middle = (slot_gain - high).astype(BF16).astype(F32)
    low = slot_gain - high - middle
    table[...] = jnp.concatenate([high, middle, low, jnp.zeros((104, 512), F32)], 0).astype(BF16)
    row = lax.broadcasted_iota(jnp.int32, (384, 128), 0)
    lane = lanes((384, 128))
    inside = jnp.zeros((384, 128), F32)
    for j, (offset, count) in enumerate(slots):
        inside = jnp.where((lane == j) & (row >= offset) & (row < offset + count), 1.0, inside)
    member[...] = inside.astype(BF16)


def add_chunk(packed, ids, sources, gram, table, member, sums):
    fourth, total = sums
    lane = lanes((256, 128))
    wanted = jnp.where(lane < 24, lane % 8, -1).astype(F32)
    value = jnp.concatenate(chunk_slots(packed, sources), 1)
    onehot = jnp.where(chunk_groups(ids, sources) == wanted, 1.0, 0.0).astype(BF16)
    gain = jnp.dot(onehot, table[...], preferred_element_type=F32)
    scaled = (value * gain[:, 0:384]).astype(BF16)
    products = lax.dot_general(
        scaled, scaled, (((0,), (0,)), ((), ())), preferred_element_type=F32
    )
    for t in range(3):
        gram[t, 0:384] += products[:, t * 128 : t * 128 + 128]
    square = value * value
    upper = square.astype(BF16)
    lower = (square - upper.astype(F32)).astype(BF16)
    norms = jnp.dot(upper, member[...], preferred_element_type=F32)
    norms += jnp.dot(lower, member[...], preferred_element_type=F32)
    weight = gain[:, 384:512] * gain[:, 384:512]
    fourth += jnp.sum(weight * norms * norms, 0, keepdims=True)
    total += jnp.sum(weight, 0, keepdims=True)
    return fourth, total


def gather_grams(slots, gram, sums, out):
    fourth, total = sums
    row = lax.broadcasted_iota(jnp.int32, (128, 128), 0)
    lane = lanes((128, 128))
    squares = []
    for offset, count in slots:
        tiles = [gram[t, pl.ds(offset, 128)] for t in range(3)]
        squares.append(jnp.where(row < count, pick_slots(tiles, lane, offset, count), 0.0))
    for half in range(2):
        upper, lower = squares[half * 2], squares[half * 2 + 1]
        out[half, 0:128] = jnp.where(row <= lane, upper, lower)
        diagonal = jnp.sum(jnp.where(row == lane, lower, 0.0), 0, keepdims=True)
        out[half, 128:136] = jnp.concatenate(
            [diagonal, fourth, total, jnp.zeros((5, 128), F32)], 0
        )


def split(value):
    high = value.astype(BF16)
    return high, (value - high.astype(F32)).astype(BF16)


def right_side(value):
    high, low = split(value)
    return jnp.concatenate(
        [jnp.concatenate([high, low], 1), jnp.concatenate([high, jnp.zeros_like(high)], 1)], 0
    )


def product(left, right):
    high, low = split(left)
    wide = jnp.dot(jnp.concatenate([high, low], 1), right, preferred_element_type=F32)
    return wide[:, 0:128] + wide[:, 128:256]


def total_of(value):
    return jnp.sum(jnp.sum(value, 0, keepdims=True), 1, keepdims=True)


def main_kernel(
    images, counts, gains, noise, coeffs, my_ids, out,
    packed, arrived, cleaned, returned, all_ids, ids, gram, table, member,
    part, other, mine, parts, cov_ref, cov_right, size, trace,
    my_filters, other_filters, shifted, filters,
    local, send, recv, send_ids, recv_ids, send_back, recv_back, send_sum, recv_sum,
):
    x, y, z, core = place()
    me = owner_index(x, y, z)
    quarter, low = z // 2, z % 2
    slots = block_slots(counts, me * 4)
    partner = {"img": y * 8 + z, "grp": x * 2 + 1 - core}
    column = []
    for step in (2, 1, 3):
        column.append({"img": y * 8 + (quarter + step) % 4 * 2 + low, "grp": x * 2 + core})
    barrier = pltpu.get_barrier_semaphore()
    for device in [peer_of(i, 1)[0] for i in range(31)] + [partner] + column:
        pl.semaphore_signal(barrier, inc=1, device_id=device, device_id_type=MESH_ID)

    def remote(source, target, sent, received, device):
        return pltpu.make_async_remote_copy(
            source, target, sent, received, device_id=device, device_id_type=MESH_ID
        )

    def data_copy(i):
        device, index = peer_of(i, 1)
        return remote(packed.at[index], arrived.at[me], send.at[i], recv.at[i], device)

    def ids_copy(i):
        return remote(my_ids, all_ids.at[me], send_ids.at[i], recv_ids.at[i], peer_of(i, 1)[0])

    def back_copy(i):
        device, index = peer_of(i, 1)
        return remote(cleaned.at[index], returned.at[me], send_back.at[i], recv_back.at[i], device)

    def sum_copy(source, target, i, device):
        return remote(source, target, send_sum.at[i], recv_sum.at[i], device)

    @pl.loop(0, 20)
    def _(i):
        pack_block(counts, coeffs, peer_of(i, 1)[1], packed)

    make_tables(slots, gains, me * 4, gram, table, member)
    pl.semaphore_wait(barrier, 35)

    @pl.loop(0, 31)
    def _(i):
        ids_copy(i).start()

    @pl.loop(0, 20)
    def _(i):
        data_copy(i).start()

    @pl.loop(20, 32)
    def _(i):
        pack_block(counts, coeffs, peer_of(i, 1)[1], packed)

        @pl.when(i < 31)
        def _():
            data_copy(i).start()

    own = pltpu.make_async_copy(packed.at[me], arrived.at[me], local.at[0])
    own.start()
    own_ids = pltpu.make_async_copy(my_ids, all_ids.at[me], local.at[1])
    own_ids.start()
    own_ids.wait()

    @pl.loop(0, 31)
    def _(i):
        ids_copy(i).wait()

    wide = jnp.concatenate([all_ids[s] for s in range(32)], 0).astype(F32)
    ids[...] = jnp.concatenate([wide, jnp.zeros((96, 128), F32)], 0).T[0:32]
    own.wait()

    def chunk(m, sums):
        sources = []
        for s in range(4):
            i = m * 4 + s
            if s < 3:
                data_copy(i).wait_recv()
            else:

                @pl.when(i < 31)
                def _():
                    data_copy(i).wait_recv()

            sources.append(peer_of(i, -1)[1])
        return add_chunk(arrived, ids, sources, gram, table, member, sums)

    nothing = jnp.zeros((1, 128), F32)
    gather_grams(slots, gram, lax.fori_loop(0, 8, chunk, (nothing, nothing)), part)

    swap = sum_copy(part.at[1 - core], other, 0, partner)
    swap.start()
    swap.wait()
    both = part[core] + other[...]
    mine[...] = both
    copies = [sum_copy(mine, parts.at[quarter], i + 1, d) for i, d in enumerate(column)]
    for copy in copies:
        copy.start()
    parts[quarter] = both
    for copy in copies:
        copy.wait()
    make_covariances(images, counts, parts, cov_ref, cov_right, size, trace)

    def send_pair(pair):
        groups = pl.ds(pair * 2, 2)
        return sum_copy(my_filters.at[groups], other_filters.at[groups], pair + 4, partner)

    @pl.loop(0, 4)
    def _(pair):
        make_filters(pair, gains, noise, my_filters, cov_ref, cov_right, size, trace)
        send_pair(pair).start()

    shifted[...] = jnp.zeros_like(shifted)

    @pl.loop(0, 4)
    def _(pair):
        send_pair(pair).wait()
        for half in range(2):
            place_filters(slots, pair * 2 + half, my_filters, other_filters, shifted, filters)

    @pl.loop(0, 8)
    def _(m):
        apply_chunk(arrived, ids, [peer_of(m * 4 + s, 1)[1] for s in range(4)], filters, cleaned)
        for s in range(4):
            i = m * 4 + s
            if s < 3:
                back_copy(i).start()
            else:

                @pl.when(i < 31)
                def _():
                    back_copy(i).start()

    unpack_block(counts, cleaned, me, out)

    @pl.loop(0, 31)
    def _(i):
        back_copy(i).wait_recv()
        unpack_block(counts, returned, peer_of(i, -1)[1], out)

    @pl.loop(0, 31)
    def _(i):
        data_copy(i).wait_send()
        back_copy(i).wait_send()


def make_covariances(images, counts, parts, cov_ref, cov_right, size, trace):
    x, y, z, core = place()
    first_freq = owner_index(x, y, z) * 4 + core * 2
    row = lax.broadcasted_iota(jnp.int32, (128, 128), 0)
    lane = lanes((128, 128))
    line = lanes((1, 128))
    block = ((parts[0] + parts[1]) + parts[2]) + parts[3]
    square = block[0:128]
    above = jnp.where(row < lane, square, 0.0)
    below = jnp.where(row > lane, square, 0.0)
    grams = (
        jnp.where(row <= lane, square, 0.0) + above.T,
        jnp.where(row == lane, block[128:129], below) + below.T,
    )
    for j in range(2):
        count = counts[first_freq + j]
        here = line == core * 2 + j
        fourth = jnp.sum(jnp.where(here, block[129:130], 0.0), 1, keepdims=True)
        total = jnp.sum(jnp.where(here, block[130:131], 0.0), 1, keepdims=True)
        sample = grams[j] / total
        ident = jnp.where((row == lane) & (row < count), 1.0, 0.0)
        level = total_of(sample * ident) / count.astype(F32)
        off_level = sample - level * ident
        spread = total_of(off_level * off_level)
        excess = (fourth / total - total_of(sample * sample)) / (2.0 * images)
        weight = excess / (excess + spread)
        cov = (1.0 - weight) * sample + (weight * level) * ident
        cov_ref[j] = cov
        cov_right[j] = right_side(cov)
        size[j] = jnp.broadcast_to(total_of(cov * cov), (8, 128))
        trace[j] = jnp.broadcast_to(total_of(cov * ident), (8, 128))


def make_filters(pair, gains, noise, out, cov_ref, cov_right, size, trace):
    x, y, z, core = place()
    first_freq = owner_index(x, y, z) * 4 + core * 2
    ident = jnp.where(
        lax.broadcasted_iota(jnp.int32, (128, 128), 0) == lanes((128, 128)), 1.0, 0.0
    )
    problems = [(pair * 2 + g, j) for g in range(2) for j in range(2)]
    powers, sums, scales = [], [], []
    for g, j in problems:
        gain, level = gains[g, first_freq + j], noise[first_freq + j]
        square = gain * gain
        norm = size[j, 0:1, 0:1] * (square * square)
        norm += trace[j, 0:1, 0:1] * (2.0 * square * level) + 128.0 * level * level
        scale = 1.0 / jnp.sqrt(norm)
        power = (1.0 - scale * level) * ident - (scale * square) * cov_ref[j]
        powers.append(power)
        sums.append(ident + power)
        scales.append(scale * gain)
    powers = [product(p, right_side(p)) for p in powers]
    for _ in range(NS_ITERS - 2):
        sides = [right_side(p) for p in powers]
        both = [product(jnp.concatenate([s, p], 0), r) for s, p, r in zip(sums, powers, sides)]
        sums = [s + b[0:128] for s, b in zip(sums, both)]
        powers = [b[128:256] for b in both]
    sums = [s + product(s, right_side(p)) for s, p in zip(sums, powers)]
    for (g, j), s, scale in zip(problems, sums, scales):
        out[g, j] = (scale * product(s, cov_right[j])).astype(BF16)


def place_filters(slots, g, mine, other, shifted, filters):
    core = place()[3]
    lane = lanes((128, 128))
    tiles = [[jnp.zeros((128, 128), F32)] * 3 for _ in range(3)]
    for j, (offset, count) in enumerate(slots):
        value = jnp.where(core == j // 2, mine[g, j % 2].astype(F32), other[g, j % 2].astype(F32))
        shifted[j, 128:256] = pltpu.roll(value, offset % 128, 1)
        for r in range(3):
            start = jnp.clip(r * 128 + 128 - offset, 0, 256)
            rows = shifted[j, pl.ds(start, 128)]
            for t in range(3):
                tiles[r][t] += jnp.where(slot_mask(lane, t, offset, count), rows, 0.0)
    for r in range(3):
        row = pl.ds(pl.multiple_of(g * 384 + r * 128, 128), 128)
        for t in range(3):
            filters[row, t * 128 : t * 128 + 128] = tiles[r][t].astype(BF16)


def apply_chunk(packed, ids, sources, filters, out):
    value = jnp.concatenate(chunk_slots(packed, sources), 1).astype(BF16)
    group = chunk_groups(ids, sources)
    pieces = []
    for g in range(8):
        mask = jnp.where(group == float(g), 1.0, 0.0).astype(BF16)
        pieces.append(value * jnp.concatenate([mask] * 3, 1))
    cleaned = jnp.dot(jnp.concatenate(pieces, 1), filters[...], preferred_element_type=F32)
    for s, source in enumerate(sources):
        rows = cleaned[s * 64 : s * 64 + 64]
        fold_slots(rows[:, 0:128], rows[:, 128:256], rows[:, 256:384], out.at[source])


def dft_tables(angles, freqs):
    angle_index = jnp.arange(angles, dtype=jnp.int32)
    freq_index = jnp.arange(freqs, dtype=jnp.int32)
    turns = angle_index[:, None] * freq_index[None, :] % angles
    phases = turns.astype(jnp.float32) * (2.0 * math.pi / angles)
    factor = 1.0 / math.sqrt(angles)
    cosine = jnp.cos(phases) * factor
    sine = -jnp.sin(phases) * factor
    forward = jnp.concatenate([cosine, sine], 1).astype(jnp.bfloat16)
    doubling = jnp.where(freq_index == 0, 1.0, 2.0).astype(jnp.float32)
    inverse = jnp.concatenate([cosine * doubling[None, :], sine * doubling[None, :]], 1).T.astype(
        jnp.bfloat16
    )
    return (forward, inverse)


def body(images, group_ids, counts, radial_basis, ctf_gain, noise_var):
    local_images, radii, angles = images.shape
    freqs = radial_basis.shape[0]
    image_total = local_images * lax.axis_size("img") * lax.axis_size("grp")
    dma = pltpu.SemaphoreType.DMA
    forward, inverse = dft_tables(angles, freqs)
    spectrum = jnp.dot(
        images.reshape(local_images * radii, angles), forward, preferred_element_type=F32
    )
    spectrum = spectrum.astype(BF16).reshape(local_images, radii, 2, freqs)
    coeffs = jnp.einsum(
        "nrck,krp->kcnp", spectrum, radial_basis, preferred_element_type=F32
    ).astype(BF16).reshape(freqs, 64, 128)
    ids = jnp.pad(group_ids, (0, 96)).reshape(1, 128)
    data = pltpu.VMEM((32, 160, 128), BF16)
    sums = pltpu.VMEM((136, 128), F32)
    pairs = pltpu.VMEM((8, 2, 128, 128), BF16)
    small = pltpu.VMEM((2, 8, 128), F32)
    spread = pl.pallas_call(
        functools.partial(main_kernel, image_total),
        out_shape=jax.ShapeDtypeStruct((freqs, 64, 128), BF16),
        in_specs=[SMEM, SMEM, SMEM, VMEM, VMEM],
        out_specs=VMEM,
        scratch_shapes=[
            data, data, data, data,
            pltpu.VMEM((32, 1, 128), jnp.int32), pltpu.VMEM((32, 128), F32),
            pltpu.VMEM((3, 512, 128), F32), pltpu.VMEM((128, 512), BF16),
            pltpu.VMEM((384, 128), BF16),
            pltpu.VMEM((2, 136, 128), F32), sums, sums, pltpu.VMEM((4, 136, 128), F32),
            pltpu.VMEM((2, 128, 128), F32), pltpu.VMEM((2, 256, 256), BF16), small, small,
            pairs, pairs, pltpu.VMEM((4, 384, 128), F32), pltpu.VMEM((3072, 384), BF16),
            dma((2,)), dma((31,)), dma((31,)), dma((31,)), dma((31,)), dma((31,)), dma((31,)),
            dma((8,)), dma((8,)),
        ],
        compiler_params=pltpu.CompilerParams(collective_id=0, has_side_effects=True),
        name="denoise",
    )(counts, ctf_gain, noise_var, coeffs, ids).reshape(freqs, 2, local_images, 128)
    back = jnp.einsum(
        "kcnp,krp->nrck", spread, radial_basis, preferred_element_type=F32
    ).astype(BF16)
    back = back.reshape(local_images * radii, 2 * freqs)
    denoised = jnp.dot(back, inverse, preferred_element_type=F32).astype(BF16)
    return denoised.reshape(local_images, radii, angles)


def solution(mesh):
    placed = (P(("img", "grp"), None, None), P(("img", "grp")), P(), P(), P(), P())
    return jax.shard_map(
        body, mesh=mesh, in_specs=placed, out_specs=P(("img", "grp"), None, None), check_vma=False
    )
```

```python
import functools
import math

import jax
import jax.numpy as jnp
import numpy as np
from jax import lax
from jax.experimental import pallas as pl
from jax.experimental.pallas import tpu as pltpu
from jax.sharding import PartitionSpec as P

NS_ITERS = 7
SIDE = 4
MESH_ID = pl.DeviceIdType.MESH
VMEM = pl.BlockSpec(memory_space=pltpu.VMEM)
SMEM = pl.BlockSpec(memory_space=pltpu.SMEM)
F32 = jnp.float32
BF16 = jnp.bfloat16


def place():
    img = lax.axis_index("img")
    grp = lax.axis_index("grp")
    return grp // 2, img // 8, img % 8, grp % 2


def owner_index(x, y, z):
    return x * 8 + y * 2 + z % 2


def step_of(i):
    turn = i % 4
    return (turn + 1) % 4, (i // 4 + turn + 2) % 4, 1 - i // 16


def peer_of(i, sign):
    x, y, z, core = place()
    a, b, c = step_of(i)
    px, py = (x + SIDE + sign * a) % SIDE, (y + SIDE + sign * b) % SIDE
    pz = z // 2 * 2 + (z + c) % 2
    return {"img": py * 8 + pz, "grp": px * 2 + core}, owner_index(px, py, pz)


def lanes(shape):
    return lax.broadcasted_iota(jnp.int32, shape, len(shape) - 1)


def tile(index):
    return pl.ds(pl.multiple_of(index * 128, 128), 128)


def block_slots(counts, first):
    offsets, offset = [], 0
    for j in range(4):
        count = counts[first + j]
        offsets.append((offset, count))
        offset = offset + count
    return offsets


def slot_mask(lane, t, offset, count):
    slot = lane + t * 128
    return (slot >= offset) & (slot < offset + count)


def pack_block(counts, spectrum, basis, block, out):
    lane = lanes((64, 128))
    tiles = [jnp.zeros((64, 128), F32) for _ in range(3)]
    for j, (offset, count) in enumerate(block_slots(counts, block * 4)):
        freq = block * 4 + j
        rows = [spectrum[pl.ds(pl.multiple_of((c * 128 + freq) * 32, 32), 32), :] for c in range(2)]
        coeffs = jnp.dot(
            jnp.concatenate(rows, 0).astype(BF16), basis[freq], preferred_element_type=F32
        )
        turned = pltpu.roll(coeffs, offset % 128, 1)
        tiles = [
            jnp.where(slot_mask(lane, t, offset, count), turned, tiles[t]) for t in range(3)
        ]
    fold_slots(*tiles, out.at[block])


def fold_slots(low, middle, high, out):
    out[0:64] = low.astype(BF16)
    out[64:128] = middle.astype(BF16)
    lane = lanes((32, 128))
    out[128:160] = jnp.where(lane < 64, high[0:32], pltpu.roll(high[32:64], 64, 1)).astype(BF16)


def unfold_slots(high):
    lane = lanes((32, 128))
    high = high.astype(F32)
    first = jnp.where(lane < 64, high, 0.0)
    second = jnp.where(lane < 64, pltpu.roll(high, 64, 1), 0.0)
    return jnp.concatenate([first, second], 0)


def pick_slots(tiles, lane, offset, count):
    picked = jnp.zeros_like(tiles[0])
    for t in range(3):
        picked = jnp.where(slot_mask(lane, t, offset, count), tiles[t], picked)
    return pltpu.roll(picked, (128 - offset % 128) % 128, 1)


def unpack_block(counts, packed, basis, block, out):
    lane = lanes((64, 128))
    tiles = [
        packed[block, 0:64].astype(F32),
        packed[block, 64:128].astype(F32),
        unfold_slots(packed[block, 128:160]),
    ]
    for j, (offset, count) in enumerate(block_slots(counts, block * 4)):
        freq = block * 4 + j
        cleaned = pick_slots(tiles, lane, offset, count).astype(BF16)
        back = lax.dot_general(
            cleaned, basis[freq], (((1,), (1,)), ((), ())), preferred_element_type=F32
        ).astype(BF16)
        for c in range(2):
            out[c * 128 + freq] = back[c * 32 : c * 32 + 32]


def chunk_slots(packed, sources):
    rows = [packed[s] for s in sources]
    low = jnp.concatenate([r[0:64] for r in rows], 0).astype(F32)
    middle = jnp.concatenate([r[64:128] for r in rows], 0).astype(F32)
    high = jnp.concatenate([unfold_slots(r[128:160]) for r in rows], 0)
    return low, middle, high


def chunk_groups(ids, sources):
    rows = []
    for s in sources:
        column = pltpu.roll(ids[...], (128 - s) % 128, 1)[:, 0:1]
        rows += [jnp.broadcast_to(column, (32, 128))] * 2
    return jnp.concatenate(rows, 0)


def make_tables(slots, gains, first_freq, gram, table, member):
    gram[...] = jnp.zeros_like(gram)
    row = lax.broadcasted_iota(jnp.int32, (8, 512), 0)
    lane = lanes((8, 512))
    slot_gain = jnp.zeros((8, 512), F32)
    for j, (offset, count) in enumerate(slots):
        column = jnp.zeros((8, 512), F32)
        for g in range(8):
            column = jnp.where(row == g, gains[g, first_freq + j], column)
        here = ((lane >= offset) & (lane < offset + count)) | (lane == 384 + j)
        slot_gain = jnp.where(here, column, slot_gain)
    high = slot_gain.astype(BF16).astype(F32)
    middle = (slot_gain - high).astype(BF16).astype(F32)
    low = slot_gain - high - middle
    table[...] = jnp.concatenate([high, middle, low, jnp.zeros((104, 512), F32)], 0).astype(BF16)
    row = lax.broadcasted_iota(jnp.int32, (384, 128), 0)
    lane = lanes((384, 128))
    inside = jnp.zeros((384, 128), F32)
    for j, (offset, count) in enumerate(slots):
        inside = jnp.where((lane == j) & (row >= offset) & (row < offset + count), 1.0, inside)
    member[...] = inside.astype(BF16)


def add_chunk(packed, ids, sources, gram, table, member, sums):
    fourth, total = sums
    lane = lanes((256, 128))
    wanted = jnp.where(lane < 24, lane % 8, -1).astype(F32)
    value = jnp.concatenate(chunk_slots(packed, sources), 1)
    onehot = jnp.where(chunk_groups(ids, sources) == wanted, 1.0, 0.0).astype(BF16)
    gain = jnp.dot(onehot, table[...], preferred_element_type=F32)
    scaled = (value * gain[:, 0:384]).astype(BF16)
    products = lax.dot_general(
        scaled, scaled, (((0,), (0,)), ((), ())), preferred_element_type=F32
    )
    for t in range(3):
        gram[t, 0:384] += products[:, t * 128 : t * 128 + 128]
    square = value * value
    upper = square.astype(BF16)
    lower = (square - upper.astype(F32)).astype(BF16)
    norms = jnp.dot(upper, member[...], preferred_element_type=F32)
    norms += jnp.dot(lower, member[...], preferred_element_type=F32)
    weight = gain[:, 384:512] * gain[:, 384:512]
    fourth += jnp.sum(weight * norms * norms, 0, keepdims=True)
    total += jnp.sum(weight, 0, keepdims=True)
    return fourth, total


def gather_grams(slots, gram, sums, out):
    fourth, total = sums
    row = lax.broadcasted_iota(jnp.int32, (128, 128), 0)
    lane = lanes((128, 128))
    squares = []
    for offset, count in slots:
        tiles = [gram[t, pl.ds(offset, 128)] for t in range(3)]
        squares.append(jnp.where(row < count, pick_slots(tiles, lane, offset, count), 0.0))
    for half in range(2):
        upper, lower = squares[half * 2], squares[half * 2 + 1]
        out[half, 0:128] = jnp.where(row <= lane, upper, lower)
        diagonal = jnp.sum(jnp.where(row == lane, lower, 0.0), 0, keepdims=True)
        out[half, 128:136] = jnp.concatenate(
            [diagonal, fourth, total, jnp.zeros((5, 128), F32)], 0
        )


def split(value):
    high = value.astype(BF16)
    return high, (value - high.astype(F32)).astype(BF16)


def right_side(value):
    high, low = split(value)
    return jnp.concatenate(
        [jnp.concatenate([high, low], 1), jnp.concatenate([high, jnp.zeros_like(high)], 1)], 0
    )


def product(left, right):
    high, low = split(left)
    wide = jnp.dot(jnp.concatenate([high, low], 1), right, preferred_element_type=F32)
    return wide[:, 0:128] + wide[:, 128:256]


def total_of(value):
    return jnp.sum(jnp.sum(value, 0, keepdims=True), 1, keepdims=True)


def main_kernel(
    image_total, counts, gains, noise, images, basis_in, forward, my_ids, out,
    pixels, spectrum, basis, packed, arrived, cleaned, returned, all_ids, ids, gram, table, member,
    part, other, mine, parts, cov_ref, cov_right, size, trace,
    my_filters, other_filters, shifted, filters,
    local, load, load_basis, send, recv, send_ids, recv_ids, send_back, recv_back, send_sum, recv_sum,
):
    x, y, z, core = place()
    me = owner_index(x, y, z)
    quarter, low = z // 2, z % 2
    slots = block_slots(counts, me * 4)

    def image_copy(m):
        rows = pl.ds(pl.multiple_of(m * 512, 512), 512)
        return pltpu.make_async_copy(images.at[rows], pixels.at[rows], load.at[m])

    def basis_copy(i):
        freqs = pl.ds(peer_of(i, 1)[1] * 4, 4)
        return pltpu.make_async_copy(basis_in.at[freqs], basis.at[freqs], load_basis.at[i])

    for m in range(8):
        image_copy(m).start()
    partner = {"img": y * 8 + z, "grp": x * 2 + 1 - core}
    column = []
    for step in (2, 1, 3):
        column.append({"img": y * 8 + (quarter + step) % 4 * 2 + low, "grp": x * 2 + core})
    barrier = pltpu.get_barrier_semaphore()
    for device in [peer_of(i, 1)[0] for i in range(31)] + [partner] + column:
        pl.semaphore_signal(barrier, inc=1, device_id=device, device_id_type=MESH_ID)

    def remote(source, target, sent, received, device):
        return pltpu.make_async_remote_copy(
            source, target, sent, received, device_id=device, device_id_type=MESH_ID
        )

    def data_copy(i):
        device, index = peer_of(i, 1)
        return remote(packed.at[index], arrived.at[me], send.at[i], recv.at[i], device)

    def ids_copy(i):
        return remote(my_ids, all_ids.at[me], send_ids.at[i], recv_ids.at[i], peer_of(i, 1)[0])

    def back_copy(i):
        device, index = peer_of(i, 1)
        return remote(cleaned.at[index], returned.at[me], send_back.at[i], recv_back.at[i], device)

    def sum_copy(source, target, i, device):
        return remote(source, target, send_sum.at[i], recv_sum.at[i], device)

    @pl.loop(0, 32)
    def _(i):
        basis_copy(i).start()

    make_tables(slots, gains, me * 4, gram, table, member)

    @pl.loop(0, 8)
    def _(m):
        image_copy(m).wait()
        rows = pl.ds(pl.multiple_of(m * 512, 512), 512)
        lines = lax.dot_general(
            forward[...], pixels[rows, :], (((1,), (1,)), ((), ())), preferred_element_type=F32
        )
        for n in range(4):
            spectrum[pl.ds(m * 4 + n, 256, stride=32), :] = lines[:, n * 128 : n * 128 + 128]

    pl.semaphore_wait(barrier, 35)

    @pl.loop(0, 31)
    def _(i):
        ids_copy(i).start()

    @pl.loop(0, 16)
    def _(pair):
        for half in range(2):
            i = pair * 2 + half
            basis_copy(i).wait()
        for half in range(2):
            pack_block(counts, spectrum, basis, peer_of(pair * 2 + half, 1)[1], packed)

        data_copy(pair * 2).start()

        @pl.when(pair < 15)
        def _():
            data_copy(pair * 2 + 1).start()

    own = pltpu.make_async_copy(packed.at[me], arrived.at[me], local.at[0])
    own.start()
    own_ids = pltpu.make_async_copy(my_ids, all_ids.at[me], local.at[1])
    own_ids.start()
    own_ids.wait()

    @pl.loop(0, 31)
    def _(i):
        ids_copy(i).wait()

    wide = jnp.concatenate([all_ids[s] for s in range(32)], 0).astype(F32)
    ids[...] = jnp.concatenate([wide, jnp.zeros((96, 128), F32)], 0).T[0:32]
    own.wait()

    def chunk(m, sums):
        sources = []
        for s in range(4):
            i = m * 4 + s
            if s < 3:
                data_copy(i).wait_recv()
            else:

                @pl.when(i < 31)
                def _():
                    data_copy(i).wait_recv()

            sources.append(peer_of(i, -1)[1])
        return add_chunk(arrived, ids, sources, gram, table, member, sums)

    nothing = jnp.zeros((1, 128), F32)
    gather_grams(slots, gram, lax.fori_loop(0, 8, chunk, (nothing, nothing)), part)

    swap = sum_copy(part.at[1 - core], other, 0, partner)
    swap.start()
    swap.wait()
    both = part[core] + other[...]
    mine[...] = both
    copies = [sum_copy(mine, parts.at[quarter], i + 1, d) for i, d in enumerate(column)]
    for copy in copies:
        copy.start()
    parts[quarter] = both
    for copy in copies:
        copy.wait()
    make_covariances(image_total, counts, parts, cov_ref, cov_right, size, trace)

    def send_pair(pair):
        groups = pl.ds(pair * 2, 2)
        return sum_copy(my_filters.at[groups], other_filters.at[groups], pair + 4, partner)

    @pl.loop(0, 4)
    def _(pair):
        make_filters(pair, gains, noise, my_filters, cov_ref, cov_right, size, trace)
        send_pair(pair).start()

    shifted[...] = jnp.zeros_like(shifted)

    @pl.loop(0, 4)
    def _(pair):
        send_pair(pair).wait()
        for half in range(2):
            place_filters(slots, pair * 2 + half, my_filters, other_filters, shifted, filters)

    @pl.loop(0, 8)
    def _(m):
        apply_chunk(arrived, ids, [peer_of(m * 4 + s, 1)[1] for s in range(4)], filters, cleaned)
        for s in range(4):
            i = m * 4 + s
            if s < 3:
                back_copy(i).start()
            else:

                @pl.when(i < 31)
                def _():
                    back_copy(i).start()

    unpack_block(counts, cleaned, basis, me, out)

    @pl.loop(0, 15)
    def _(pair):
        for half in range(2):
            back_copy(pair * 2 + half).wait_recv()
        for half in range(2):
            unpack_block(counts, returned, basis, peer_of(pair * 2 + half, -1)[1], out)

    back_copy(30).wait_recv()
    unpack_block(counts, returned, basis, peer_of(30, -1)[1], out)

    @pl.loop(0, 31)
    def _(i):
        data_copy(i).wait_send()
        back_copy(i).wait_send()


def make_covariances(images, counts, parts, cov_ref, cov_right, size, trace):
    x, y, z, core = place()
    first_freq = owner_index(x, y, z) * 4 + core * 2
    row = lax.broadcasted_iota(jnp.int32, (128, 128), 0)
    lane = lanes((128, 128))
    line = lanes((1, 128))
    block = ((parts[0] + parts[1]) + parts[2]) + parts[3]
    square = block[0:128]
    above = jnp.where(row < lane, square, 0.0)
    below = jnp.where(row > lane, square, 0.0)
    grams = (
        jnp.where(row <= lane, square, 0.0) + above.T,
        jnp.where(row == lane, block[128:129], below) + below.T,
    )
    for j in range(2):
        count = counts[first_freq + j]
        here = line == core * 2 + j
        fourth = jnp.sum(jnp.where(here, block[129:130], 0.0), 1, keepdims=True)
        total = jnp.sum(jnp.where(here, block[130:131], 0.0), 1, keepdims=True)
        sample = grams[j] / total
        ident = jnp.where((row == lane) & (row < count), 1.0, 0.0)
        level = total_of(sample * ident) / count.astype(F32)
        off_level = sample - level * ident
        spread = total_of(off_level * off_level)
        excess = (fourth / total - total_of(sample * sample)) / (2.0 * images)
        weight = excess / (excess + spread)
        cov = (1.0 - weight) * sample + (weight * level) * ident
        right = right_side(cov)
        square = product(cov, right)
        cov_ref[j, 0] = cov
        cov_ref[j, 1] = square
        cov_ref[j, 2] = product(square, right)
        cov_right[j] = right
        size[j] = jnp.broadcast_to(total_of(cov * cov), (8, 128))
        trace[j] = jnp.broadcast_to(total_of(cov * ident), (8, 128))


def make_filters(pair, gains, noise, out, cov_ref, cov_right, size, trace):
    x, y, z, core = place()
    first_freq = owner_index(x, y, z) * 4 + core * 2
    ident = jnp.where(
        lax.broadcasted_iota(jnp.int32, (128, 128), 0) == lanes((128, 128)), 1.0, 0.0
    )
    problems = [(pair * 2 + g, j) for g in range(2) for j in range(2)]
    powers, sums, scales = [], [], []
    for g, j in problems:
        gain, level = gains[g, first_freq + j], noise[first_freq + j]
        square = gain * gain
        norm = size[j, 0:1, 0:1] * (square * square)
        norm += trace[j, 0:1, 0:1] * (2.0 * square * level) + 128.0 * level * level
        scale = 1.0 / jnp.sqrt(norm)
        keep, slope = 1.0 - scale * level, scale * square
        first, second, third = cov_ref[j, 0], cov_ref[j, 1], cov_ref[j, 2]
        power = keep * ident - slope * first
        twice = keep * keep * ident - (2.0 * keep * slope) * first + slope * slope * second
        thrice = (
            keep * keep * keep * ident - (3.0 * keep * keep * slope) * first
            + (3.0 * keep * slope * slope) * second - slope * slope * slope * third
        )
        powers.append(twice)
        sums.append(ident + power + twice + thrice)
        scales.append(scale * gain)
    powers = [product(p, right_side(p)) for p in powers]
    for _ in range(NS_ITERS - 3):
        sides = [right_side(p) for p in powers]
        both = [product(jnp.concatenate([s, p], 0), r) for s, p, r in zip(sums, powers, sides)]
        sums = [s + b[0:128] for s, b in zip(sums, both)]
        powers = [b[128:256] for b in both]
    sums = [s + product(s, right_side(p)) for s, p in zip(sums, powers)]
    for (g, j), s, scale in zip(problems, sums, scales):
        out[g, j] = (scale * product(s, cov_right[j])).astype(BF16)


def place_filters(slots, g, mine, other, shifted, filters):
    core = place()[3]
    lane = lanes((128, 128))
    tiles = [[jnp.zeros((128, 128), F32)] * 3 for _ in range(3)]
    for j, (offset, count) in enumerate(slots):
        value = jnp.where(core == j // 2, mine[g, j % 2].astype(F32), other[g, j % 2].astype(F32))
        shifted[j, 128:256] = pltpu.roll(value, offset % 128, 1)
        for r in range(3):
            start = jnp.clip(r * 128 + 128 - offset, 0, 256)
            rows = shifted[j, pl.ds(start, 128)]
            for t in range(3):
                tiles[r][t] += jnp.where(slot_mask(lane, t, offset, count), rows, 0.0)
    for r in range(3):
        row = pl.ds(pl.multiple_of(g * 384 + r * 128, 128), 128)
        for t in range(3):
            filters[row, t * 128 : t * 128 + 128] = tiles[r][t].astype(BF16)


def apply_chunk(packed, ids, sources, filters, out):
    value = jnp.concatenate(chunk_slots(packed, sources), 1).astype(BF16)
    group = chunk_groups(ids, sources)
    pieces = []
    for g in range(8):
        mask = jnp.where(group == float(g), 1.0, 0.0).astype(BF16)
        pieces.append(value * jnp.concatenate([mask] * 3, 1))
    cleaned = jnp.dot(jnp.concatenate(pieces, 1), filters[...], preferred_element_type=F32)
    for s, source in enumerate(sources):
        rows = cleaned[s * 64 : s * 64 + 64]
        fold_slots(rows[:, 0:128], rows[:, 128:256], rows[:, 256:384], out.at[source])


def dft_tables(angles, freqs):
    angle_index, freq_index = np.arange(angles), np.arange(freqs)
    turns = angle_index[:, None] * freq_index[None, :] % angles
    phases = turns.astype(np.float32) * np.float32(2.0 * math.pi / angles)
    factor = np.float32(1.0 / math.sqrt(angles))
    cosine = np.cos(phases) * factor
    sine = -np.sin(phases) * factor
    doubling = np.where(freq_index == 0, 1.0, 2.0).astype(np.float32)
    forward = np.concatenate([cosine, sine], 1).T
    inverse = np.concatenate([cosine * doubling, sine * doubling], 1).T
    return forward.astype(BF16), inverse.astype(BF16)


def body(images, group_ids, counts, radial_basis, ctf_gain, noise_var):
    local_images, radii, angles = images.shape
    freqs = radial_basis.shape[0]
    image_total = local_images * lax.axis_size("img") * lax.axis_size("grp")
    dma = pltpu.SemaphoreType.DMA
    forward, inverse = dft_tables(angles, freqs)
    ids = jnp.pad(group_ids, (0, 96)).reshape(1, 128)
    data = pltpu.VMEM((32, 160, 128), BF16)
    sums = pltpu.VMEM((136, 128), F32)
    pairs = pltpu.VMEM((8, 2, 128, 128), BF16)
    small = pltpu.VMEM((2, 8, 128), F32)
    anywhere = pl.BlockSpec(memory_space=pl.ANY)
    back = pl.pallas_call(
        functools.partial(main_kernel, image_total),
        out_shape=jax.ShapeDtypeStruct((2 * freqs, local_images, radii), BF16),
        in_specs=[SMEM, SMEM, SMEM, anywhere, anywhere, VMEM, VMEM],
        out_specs=VMEM,
        scratch_shapes=[
            pltpu.VMEM((local_images * radii, angles), BF16),
            pltpu.VMEM((2 * freqs * local_images, radii), F32),
            pltpu.VMEM(radial_basis.shape, BF16),
            data, data, data, data,
            pltpu.VMEM((32, 1, 128), jnp.int32), pltpu.VMEM((32, 128), F32),
            pltpu.VMEM((3, 512, 128), F32), pltpu.VMEM((128, 512), BF16),
            pltpu.VMEM((384, 128), BF16),
            pltpu.VMEM((2, 136, 128), F32), sums, sums, pltpu.VMEM((4, 136, 128), F32),
            pltpu.VMEM((2, 3, 128, 128), F32), pltpu.VMEM((2, 256, 256), BF16), small, small,
            pairs, pairs, pltpu.VMEM((4, 384, 128), F32), pltpu.VMEM((3072, 384), BF16),
            dma((2,)), dma((8,)), dma((32,)),
            dma((31,)), dma((31,)), dma((31,)), dma((31,)), dma((31,)), dma((31,)),
            dma((8,)), dma((8,)),
        ],
        compiler_params=pltpu.CompilerParams(collective_id=0, has_side_effects=True),
        name="denoise",
    )(
        counts, ctf_gain, noise_var, images.reshape(local_images * radii, angles), radial_basis,
        jnp.asarray(forward), ids,
    )
    denoised = jnp.einsum("knr,ka->nra", back, jnp.asarray(inverse), preferred_element_type=F32)
    return denoised.astype(BF16)


def solution(mesh):
    placed = (P(("img", "grp"), None, None), P(("img", "grp")), P(), P(), P(), P())
    return jax.shard_map(
        body, mesh=mesh, in_specs=placed, out_specs=P(("img", "grp"), None, None), check_vma=False
    )
```

```python
import functools
import math

import jax
import jax.numpy as jnp
import numpy as np
from jax import lax
from jax.experimental import pallas as pl
from jax.experimental.pallas import tpu as pltpu
from jax.sharding import PartitionSpec as P

NS_ITERS = 7
SIDE = 4
MESH_ID = pl.DeviceIdType.MESH
VMEM = pl.BlockSpec(memory_space=pltpu.VMEM)
F32 = jnp.float32
BF16 = jnp.bfloat16


def place():
    img = lax.axis_index("img")
    grp = lax.axis_index("grp")
    return grp // 2, img // 8, img % 8, grp % 2


def owner_index(x, y, z):
    return x * 8 + y * 2 + z % 2


def step_of(i):
    turn = i % 4
    return (turn + 1) % 4, (i // 4 + turn + 2) % 4, 1 - i // 16


def peer_of(i, sign):
    x, y, z, core = place()
    a, b, c = step_of(i)
    px, py = (x + SIDE + sign * a) % SIDE, (y + SIDE + sign * b) % SIDE
    pz = z // 2 * 2 + (z + c) % 2
    return {"img": py * 8 + pz, "grp": px * 2 + core}, owner_index(px, py, pz)


def lanes(shape):
    return lax.broadcasted_iota(jnp.int32, shape, len(shape) - 1)


def tile(index):
    return pl.ds(pl.multiple_of(index * 128, 128), 128)


def block_slots(counts, first):
    offsets, offset = [], 0
    for j in range(4):
        count = counts[first + j]
        offsets.append((offset, count))
        offset = offset + count
    return offsets


def slot_mask(lane, t, offset, count):
    slot = lane + t * 128
    return (slot >= offset) & (slot < offset + count)


def pack_block(counts, spectrum, basis, block, out):
    lane = lanes((64, 128))
    tiles = [jnp.zeros((64, 128), F32) for _ in range(3)]
    for j, (offset, count) in enumerate(block_slots(counts, block * 4)):
        freq = block * 4 + j
        rows = [spectrum[pl.ds(pl.multiple_of((c * 128 + freq) * 32, 32), 32), :] for c in range(2)]
        coeffs = jnp.dot(
            jnp.concatenate(rows, 0).astype(BF16), basis[freq], preferred_element_type=F32
        )
        turned = pltpu.roll(coeffs, offset % 128, 1)
        tiles = [
            jnp.where(slot_mask(lane, t, offset, count), turned, tiles[t]) for t in range(3)
        ]
    fold_slots(*tiles, out.at[block])


def fold_slots(low, middle, high, out):
    out[0:64] = low.astype(BF16)
    out[64:128] = middle.astype(BF16)
    lane = lanes((32, 128))
    out[128:160] = jnp.where(lane < 64, high[0:32], pltpu.roll(high[32:64], 64, 1)).astype(BF16)


def unfold_slots(high):
    lane = lanes((32, 128))
    high = high.astype(F32)
    first = jnp.where(lane < 64, high, 0.0)
    second = jnp.where(lane < 64, pltpu.roll(high, 64, 1), 0.0)
    return jnp.concatenate([first, second], 0)


def pick_slots(tiles, lane, offset, count):
    picked = jnp.zeros_like(tiles[0])
    for t in range(3):
        picked = jnp.where(slot_mask(lane, t, offset, count), tiles[t], picked)
    return pltpu.roll(picked, (128 - offset % 128) % 128, 1)


def unpack_block(counts, packed, basis, block, out):
    lane = lanes((64, 128))
    tiles = [
        packed[block, 0:64].astype(F32),
        packed[block, 64:128].astype(F32),
        unfold_slots(packed[block, 128:160]),
    ]
    for j, (offset, count) in enumerate(block_slots(counts, block * 4)):
        freq = block * 4 + j
        cleaned = pick_slots(tiles, lane, offset, count).astype(BF16)
        back = lax.dot_general(
            cleaned, basis[freq], (((1,), (1,)), ((), ())), preferred_element_type=F32
        ).astype(BF16)
        for c in range(2):
            out[c * 128 + freq] = back[c * 32 : c * 32 + 32]


def chunk_slots(packed, sources):
    rows = [packed[s] for s in sources]
    low = jnp.concatenate([r[0:64] for r in rows], 0).astype(F32)
    middle = jnp.concatenate([r[64:128] for r in rows], 0).astype(F32)
    high = jnp.concatenate([unfold_slots(r[128:160]) for r in rows], 0)
    return low, middle, high


def store_groups(all_ids, groups, sources):
    rows = jnp.concatenate([all_ids[s] for s in sources], 0).astype(F32)
    rows = jnp.concatenate([rows, jnp.zeros((4, 96), F32)], 1)
    turned = jnp.concatenate([rows, jnp.zeros((124, 128), F32)], 0).T[0:32]
    for i, s in enumerate(sources):
        groups[s] = jnp.broadcast_to(turned[:, i : i + 1], (32, 128))


def chunk_groups(groups, sources):
    return jnp.concatenate([r for s in sources for r in [groups[s]] * 2], 0)


def make_tables(slots, gains, first_freq, gram, table, member):
    gram[...] = jnp.zeros_like(gram)
    row = lax.broadcasted_iota(jnp.int32, (8, 512), 0)
    lane = lanes((8, 512))
    slot_gain = jnp.zeros((8, 512), F32)
    for j, (offset, count) in enumerate(slots):
        column = jnp.zeros((8, 512), F32)
        for g in range(8):
            column = jnp.where(row == g, gains[g, first_freq + j], column)
        here = ((lane >= offset) & (lane < offset + count)) | (lane == 384 + j)
        slot_gain = jnp.where(here, column, slot_gain)
    high = slot_gain.astype(BF16).astype(F32)
    middle = (slot_gain - high).astype(BF16).astype(F32)
    low = slot_gain - high - middle
    table[...] = jnp.concatenate([high, middle, low, jnp.zeros((104, 512), F32)], 0).astype(BF16)
    row = lax.broadcasted_iota(jnp.int32, (384, 128), 0)
    lane = lanes((384, 128))
    inside = jnp.zeros((384, 128), F32)
    for j, (offset, count) in enumerate(slots):
        inside = jnp.where((lane == j) & (row >= offset) & (row < offset + count), 1.0, inside)
    member[...] = inside.astype(BF16)


def add_chunk(packed, groups, sources, gram, table, member, sums):
    fourth, total = sums
    lane = lanes((256, 128))
    wanted = jnp.where(lane < 24, lane % 8, -1).astype(F32)
    value = jnp.concatenate(chunk_slots(packed, sources), 1)
    onehot = jnp.where(chunk_groups(groups, sources) == wanted, 1.0, 0.0).astype(BF16)
    gain = jnp.dot(onehot, table[...], preferred_element_type=F32)
    scaled = (value * gain[:, 0:384]).astype(BF16)
    products = lax.dot_general(
        scaled, scaled, (((0,), (0,)), ((), ())), preferred_element_type=F32
    )
    for t in range(3):
        gram[t, 0:384] += products[:, t * 128 : t * 128 + 128]
    square = value * value
    upper = square.astype(BF16)
    lower = (square - upper.astype(F32)).astype(BF16)
    norms = jnp.dot(upper, member[...], preferred_element_type=F32)
    norms += jnp.dot(lower, member[...], preferred_element_type=F32)
    weight = gain[:, 384:512] * gain[:, 384:512]
    fourth += jnp.sum(weight * norms * norms, 0, keepdims=True)
    total += jnp.sum(weight, 0, keepdims=True)
    return fourth, total


def gather_grams(slots, gram, sums, out):
    fourth, total = sums
    row = lax.broadcasted_iota(jnp.int32, (128, 128), 0)
    lane = lanes((128, 128))
    squares = []
    for offset, count in slots:
        tiles = [gram[t, pl.ds(offset, 128)] for t in range(3)]
        squares.append(jnp.where(row < count, pick_slots(tiles, lane, offset, count), 0.0))
    for half in range(2):
        upper, lower = squares[half * 2], squares[half * 2 + 1]
        out[half, 0:128] = jnp.where(row <= lane, upper, lower)
        diagonal = jnp.sum(jnp.where(row == lane, lower, 0.0), 0, keepdims=True)
        out[half, 128:136] = jnp.concatenate(
            [diagonal, fourth, total, jnp.zeros((5, 128), F32)], 0
        )


def split(value):
    high = value.astype(BF16)
    return high, (value - high.astype(F32)).astype(BF16)


def right_side(value):
    high, low = split(value)
    return jnp.concatenate(
        [jnp.concatenate([high, low], 1), jnp.concatenate([high, jnp.zeros_like(high)], 1)], 0
    )


def product(left, right):
    high, low = split(left)
    wide = jnp.dot(jnp.concatenate([high, low], 1), right, preferred_element_type=F32)
    return wide[:, 0:128] + wide[:, 128:256]


def total_of(value):
    return jnp.sum(jnp.sum(value, 0, keepdims=True), 1, keepdims=True)


def main_kernel(
    image_total, counts_in, gains_in, noise_in, images, basis_in, forward_in, ids_in, out,
    counts, gains, noise, forward, my_ids, pixels, spectrum, basis, packed, arrived, cleaned, returned, all_ids, groups, gram, table, member,
    part, other, mine, parts, cov_ref, cov_right, size, trace,
    my_filters, other_filters, shifted, filters,
    local, load, load_basis, load_small, send, recv, send_ids, recv_ids, send_back, recv_back, send_sum, recv_sum,
):
    x, y, z, core = place()
    me = owner_index(x, y, z)
    quarter, low = z // 2, z % 2
    smalls = [(counts_in, counts), (gains_in, gains), (noise_in, noise)]
    smalls += [(forward_in, forward), (ids_in, my_ids)]
    smalls = [
        pltpu.make_async_copy(source, target, load_small.at[i])
        for i, (source, target) in enumerate(smalls)
    ]
    for copy in smalls:
        copy.start()

    def image_copy(m):
        rows = pl.ds(pl.multiple_of(m * 512, 512), 512)
        return pltpu.make_async_copy(images.at[rows], pixels.at[rows], load.at[m])

    def basis_copy(m):
        freqs = pl.ds(m * 32, 32)
        return pltpu.make_async_copy(basis_in.at[freqs], basis.at[freqs], load_basis.at[m])

    for m in range(8):
        image_copy(m).start()
    for m in range(4):
        basis_copy(m).start()
    partner = {"img": y * 8 + z, "grp": x * 2 + 1 - core}
    column = []
    for step in (2, 1, 3):
        column.append({"img": y * 8 + (quarter + step) % 4 * 2 + low, "grp": x * 2 + core})
    barrier = pltpu.get_barrier_semaphore()
    for device in [peer_of(i, 1)[0] for i in range(31)] + [partner] + column:
        pl.semaphore_signal(barrier, inc=1, device_id=device, device_id_type=MESH_ID)
    for copy in smalls:
        copy.wait()
    slots = block_slots(counts, me * 4)

    def remote(source, target, sent, received, device):
        return pltpu.make_async_remote_copy(
            source, target, sent, received, device_id=device, device_id_type=MESH_ID
        )

    def data_copy(i):
        device, index = peer_of(i, 1)
        return remote(packed.at[index], arrived.at[me], send.at[i], recv.at[i], device)

    def ids_copy(i):
        return remote(my_ids, all_ids.at[me], send_ids.at[i], recv_ids.at[i], peer_of(i, 1)[0])

    def back_copy(i):
        device, index = peer_of(i, 1)
        return remote(cleaned.at[index], returned.at[me], send_back.at[i], recv_back.at[i], device)

    def sum_copy(source, target, i, device):
        return remote(source, target, send_sum.at[i], recv_sum.at[i], device)

    @pl.loop(0, 8)
    def _(m):
        image_copy(m).wait()
        rows = pl.ds(pl.multiple_of(m * 512, 512), 512)
        lines = lax.dot_general(
            forward[...], pixels[rows, :], (((1,), (1,)), ((), ())), preferred_element_type=F32
        )
        for n in range(4):
            spectrum[pl.ds(m * 4 + n, 256, stride=32), :] = lines[:, n * 128 : n * 128 + 128]

    pl.semaphore_wait(barrier, 35)

    for m in range(4):
        basis_copy(m).wait()

    def send_block(i):
        ids_copy(i).start()
        data_copy(i).start()

    @pl.loop(0, 16)
    def _(pair):
        for half in range(2):
            pack_block(counts, spectrum, basis, peer_of(pair * 2 + half, 1)[1], packed)

        send_block(pair * 2)

        @pl.when(pair < 15)
        def _():
            send_block(pair * 2 + 1)

    own = pltpu.make_async_copy(packed.at[me], arrived.at[me], local.at[0])
    own.start()
    own_ids = pltpu.make_async_copy(my_ids, all_ids.at[me], local.at[1])
    own_ids.start()
    make_tables(slots, gains, me * 4, gram, table, member)
    own_ids.wait()
    own.wait()

    def chunk(m, sums):
        sources = []
        for s in range(4):
            i = m * 4 + s
            if s < 3:
                data_copy(i).wait_recv()
                ids_copy(i).wait_recv()
            else:

                @pl.when(i < 31)
                def _():
                    data_copy(i).wait_recv()
                    ids_copy(i).wait_recv()

            sources.append(peer_of(i, -1)[1])
        store_groups(all_ids, groups, sources)
        return add_chunk(arrived, groups, sources, gram, table, member, sums)

    nothing = jnp.zeros((1, 128), F32)
    gather_grams(slots, gram, lax.fori_loop(0, 8, chunk, (nothing, nothing)), part)

    swap = sum_copy(part.at[1 - core], other, 0, partner)
    swap.start()
    swap.wait()
    both = part[core] + other[...]
    mine[...] = both
    copies = [sum_copy(mine, parts.at[quarter], i + 1, d) for i, d in enumerate(column)]
    for copy in copies:
        copy.start()
    parts[quarter] = both
    for copy in copies:
        copy.wait()
    make_covariances(image_total, counts, parts, cov_ref, cov_right, size, trace)

    def send_pair(pair):
        groups = pl.ds(pair * 2, 2)
        return sum_copy(my_filters.at[groups], other_filters.at[groups], pair + 4, partner)

    def place_pair(pair):
        for half in range(2):
            place_filters(slots, pair * 2 + half, my_filters, other_filters, shifted, filters)

    shifted[...] = jnp.zeros_like(shifted)
    make_filters(0, gains, noise, my_filters, cov_ref, cov_right, size, trace)
    send_pair(0).start()

    @pl.loop(1, 4)
    def _(pair):
        send_pair(pair - 1).wait()
        place_pair(pair - 1)
        make_filters(pair, gains, noise, my_filters, cov_ref, cov_right, size, trace)
        send_pair(pair).start()

    send_pair(3).wait()
    place_pair(3)

    @pl.loop(0, 8)
    def _(m):
        apply_chunk(arrived, groups, [peer_of(m * 4 + s, 1)[1] for s in range(4)], filters, cleaned)
        for s in range(4):
            i = m * 4 + s
            if s < 3:
                back_copy(i).start()
            else:

                @pl.when(i < 31)
                def _():
                    back_copy(i).start()

    unpack_block(counts, cleaned, basis, me, out)

    @pl.loop(0, 15)
    def _(pair):
        for half in range(2):
            back_copy(pair * 2 + half).wait_recv()
        for half in range(2):
            unpack_block(counts, returned, basis, peer_of(pair * 2 + half, -1)[1], out)

    back_copy(30).wait_recv()
    unpack_block(counts, returned, basis, peer_of(30, -1)[1], out)

    @pl.loop(0, 31)
    def _(i):
        ids_copy(i).wait_send()
        data_copy(i).wait_send()
        back_copy(i).wait_send()


def make_covariances(images, counts, parts, cov_ref, cov_right, size, trace):
    x, y, z, core = place()
    first_freq = owner_index(x, y, z) * 4 + core * 2
    row = lax.broadcasted_iota(jnp.int32, (128, 128), 0)
    lane = lanes((128, 128))
    line = lanes((1, 128))
    block = ((parts[0] + parts[1]) + parts[2]) + parts[3]
    square = block[0:128]
    above = jnp.where(row < lane, square, 0.0)
    below = jnp.where(row > lane, square, 0.0)
    grams = (
        jnp.where(row <= lane, square, 0.0) + above.T,
        jnp.where(row == lane, block[128:129], below) + below.T,
    )
    for j in range(2):
        count = counts[first_freq + j]
        here = line == core * 2 + j
        fourth = jnp.sum(jnp.where(here, block[129:130], 0.0), 1, keepdims=True)
        total = jnp.sum(jnp.where(here, block[130:131], 0.0), 1, keepdims=True)
        sample = grams[j] / total
        ident = jnp.where((row == lane) & (row < count), 1.0, 0.0)
        level = total_of(sample * ident) / count.astype(F32)
        off_level = sample - level * ident
        spread = total_of(off_level * off_level)
        excess = (fourth / total - total_of(sample * sample)) / (2.0 * images)
        weight = excess / (excess + spread)
        cov = (1.0 - weight) * sample + (weight * level) * ident
        right = right_side(cov)
        square = product(cov, right)
        cov_ref[j, 0] = cov
        cov_ref[j, 1] = square
        cov_ref[j, 2] = product(square, right)
        cov_right[j] = right
        size[j] = jnp.broadcast_to(total_of(cov * cov), (8, 128))
        trace[j] = jnp.broadcast_to(total_of(cov * ident), (8, 128))


def make_filters(pair, gains, noise, out, cov_ref, cov_right, size, trace):
    x, y, z, core = place()
    first_freq = owner_index(x, y, z) * 4 + core * 2
    ident = jnp.where(
        lax.broadcasted_iota(jnp.int32, (128, 128), 0) == lanes((128, 128)), 1.0, 0.0
    )
    problems = [(pair * 2 + g, j) for g in range(2) for j in range(2)]
    powers, sums, scales = [], [], []
    for g, j in problems:
        gain, level = gains[g, first_freq + j], noise[first_freq + j]
        square = gain * gain
        norm = size[j, 0:1, 0:1] * (square * square)
        norm += trace[j, 0:1, 0:1] * (2.0 * square * level) + 128.0 * level * level
        scale = 1.0 / jnp.sqrt(norm)
        keep, slope = 1.0 - scale * level, scale * square
        first, second, third = cov_ref[j, 0], cov_ref[j, 1], cov_ref[j, 2]
        power = keep * ident - slope * first
        twice = keep * keep * ident - (2.0 * keep * slope) * first + slope * slope * second
        thrice = (
            keep * keep * keep * ident - (3.0 * keep * keep * slope) * first
            + (3.0 * keep * slope * slope) * second - slope * slope * slope * third
        )
        powers.append(twice)
        sums.append(ident + power + twice + thrice)
        scales.append(scale * gain)
    powers = [product(p, right_side(p)) for p in powers]
    for _ in range(NS_ITERS - 3):
        sides = [right_side(p) for p in powers]
        both = [product(jnp.concatenate([s, p], 0), r) for s, p, r in zip(sums, powers, sides)]
        sums = [s + b[0:128] for s, b in zip(sums, both)]
        powers = [b[128:256] for b in both]
    sums = [s + product(s, right_side(p)) for s, p in zip(sums, powers)]
    for (g, j), s, scale in zip(problems, sums, scales):
        out[g, j] = (scale * product(s, cov_right[j])).astype(BF16)


def place_filters(slots, g, mine, other, shifted, filters):
    core = place()[3]
    lane = lanes((128, 128))
    tiles = [[jnp.zeros((128, 128), F32)] * 3 for _ in range(3)]
    for j, (offset, count) in enumerate(slots):
        value = jnp.where(core == j // 2, mine[g, j % 2].astype(F32), other[g, j % 2].astype(F32))
        shifted[j, 128:256] = pltpu.roll(value, offset % 128, 1)
        for r in range(3):
            start = jnp.clip(r * 128 + 128 - offset, 0, 256)
            rows = shifted[j, pl.ds(start, 128)]
            for t in range(3):
                tiles[r][t] += jnp.where(slot_mask(lane, t, offset, count), rows, 0.0)
    for r in range(3):
        row = pl.ds(pl.multiple_of(g * 384 + r * 128, 128), 128)
        for t in range(3):
            filters[row, t * 128 : t * 128 + 128] = tiles[r][t].astype(BF16)


def apply_chunk(packed, groups, sources, filters, out):
    value = jnp.concatenate(chunk_slots(packed, sources), 1).astype(BF16)
    group = chunk_groups(groups, sources)
    pieces = []
    for g in range(8):
        mask = jnp.where(group == float(g), 1.0, 0.0).astype(BF16)
        pieces.append(value * jnp.concatenate([mask] * 3, 1))
    cleaned = jnp.dot(jnp.concatenate(pieces, 1), filters[...], preferred_element_type=F32)
    for s, source in enumerate(sources):
        rows = cleaned[s * 64 : s * 64 + 64]
        fold_slots(rows[:, 0:128], rows[:, 128:256], rows[:, 256:384], out.at[source])


def dft_tables(angles, freqs):
    angle_index, freq_index = np.arange(angles), np.arange(freqs)
    turns = angle_index[:, None] * freq_index[None, :] % angles
    phases = turns.astype(np.float32) * np.float32(2.0 * math.pi / angles)
    factor = np.float32(1.0 / math.sqrt(angles))
    cosine = np.cos(phases) * factor
    sine = -np.sin(phases) * factor
    doubling = np.where(freq_index == 0, 1.0, 2.0).astype(np.float32)
    forward = np.concatenate([cosine, sine], 1).T
    inverse = np.concatenate([cosine * doubling, sine * doubling], 1).T
    return forward.astype(BF16), inverse.astype(BF16)


def body(images, group_ids, counts, radial_basis, ctf_gain, noise_var):
    local_images, radii, angles = images.shape
    freqs = radial_basis.shape[0]
    image_total = local_images * lax.axis_size("img") * lax.axis_size("grp")
    dma = pltpu.SemaphoreType.DMA
    forward, inverse = dft_tables(angles, freqs)
    ids = group_ids.reshape(1, local_images)
    data = pltpu.VMEM((32, 160, 128), BF16)
    sums = pltpu.VMEM((136, 128), F32)
    pairs = pltpu.VMEM((8, 2, 128, 128), BF16)
    small = pltpu.VMEM((2, 8, 128), F32)
    hbm = pl.BlockSpec(memory_space=pltpu.HBM)
    back = pl.pallas_call(
        functools.partial(main_kernel, image_total),
        out_shape=jax.ShapeDtypeStruct((2 * freqs, local_images, radii), BF16),
        in_specs=[hbm] * 7,
        out_specs=VMEM,
        scratch_shapes=[
            pltpu.SMEM(counts.shape, jnp.int32), pltpu.SMEM(ctf_gain.shape, F32),
            pltpu.SMEM(noise_var.shape, F32), pltpu.VMEM(forward.shape, BF16),
            pltpu.VMEM(ids.shape, jnp.int32),
            pltpu.VMEM((local_images * radii, angles), BF16),
            pltpu.VMEM((2 * freqs * local_images, radii), F32),
            pltpu.VMEM(radial_basis.shape, BF16),
            data, data, data, data,
            pltpu.VMEM((32, 1, 32), jnp.int32), pltpu.VMEM((32, 32, 128), F32),
            pltpu.VMEM((3, 512, 128), F32), pltpu.VMEM((128, 512), BF16),
            pltpu.VMEM((384, 128), BF16),
            pltpu.VMEM((2, 136, 128), F32), sums, sums, pltpu.VMEM((4, 136, 128), F32),
            pltpu.VMEM((2, 3, 128, 128), F32), pltpu.VMEM((2, 256, 256), BF16), small, small,
            pairs, pairs, pltpu.VMEM((4, 384, 128), F32), pltpu.VMEM((3072, 384), BF16),
            dma((2,)), dma((8,)), dma((4,)), dma((5,)),
            dma((31,)), dma((31,)), dma((31,)), dma((31,)), dma((31,)), dma((31,)),
            dma((8,)), dma((8,)),
        ],
        compiler_params=pltpu.CompilerParams(collective_id=0, has_side_effects=True),
        name="denoise",
    )(
        counts, ctf_gain, noise_var, images.reshape(local_images * radii, angles), radial_basis,
        jnp.asarray(forward), ids,
    )
    denoised = jnp.einsum("knr,ka->nra", back, jnp.asarray(inverse), preferred_element_type=F32)
    return denoised.astype(BF16)


def solution(mesh):
    placed = (P(("img", "grp"), None, None), P(("img", "grp")), P(), P(), P(), P())
    return jax.shard_map(
        body, mesh=mesh, in_specs=placed, out_specs=P(("img", "grp"), None, None), check_vma=False
    )
```

```python
import functools
import math

import jax
import jax.numpy as jnp
import numpy as np
from jax import lax
from jax.experimental import pallas as pl
from jax.experimental.pallas import tpu as pltpu
from jax.sharding import PartitionSpec as P

NS_ITERS = 7
SIDE = 4
MESH_ID = pl.DeviceIdType.MESH
VMEM = pl.BlockSpec(memory_space=pltpu.VMEM)
F32 = jnp.float32
BF16 = jnp.bfloat16


def rem(a, n):
    return a % n if isinstance(a, int) else lax.rem(a, jnp.int32(n))


def div(a, n):
    return a // n if isinstance(a, int) else lax.div(a, jnp.int32(n))


def place():
    img = lax.axis_index("img")
    grp = lax.axis_index("grp")
    return div(grp, 2), div(img, 8), rem(img, 8), rem(grp, 2)


def owner_index(x, y, z):
    return x * 8 + y * 2 + rem(z, 2)


def step_of(i):
    turn = rem(i, 4)
    return rem(turn + 1, 4), rem(div(i, 4) + turn + 2, 4), 1 - div(i, 16)


def peer_of(i, sign):
    x, y, z, core = place()
    a, b, c = step_of(i)
    px, py = rem(x + SIDE + sign * a, SIDE), rem(y + SIDE + sign * b, SIDE)
    pz = div(z, 2) * 2 + rem(z + c, 2)
    return {"img": py * 8 + pz, "grp": px * 2 + core}, owner_index(px, py, pz)


def lanes(shape):
    return lax.broadcasted_iota(jnp.int32, shape, len(shape) - 1)


def tile(index):
    return pl.ds(pl.multiple_of(index * 128, 128), 128)


def block_slots(counts, first):
    offsets, offset = [], 0
    for j in range(4):
        count = counts[first + j]
        offsets.append((offset, count))
        offset = offset + count
    return offsets


def slot_mask(lane, t, offset, count):
    slot = lane + t * 128
    return (slot >= offset) & (slot < offset + count)


def pack_block(counts, spectrum, basis, block, out):
    lane = lanes((64, 128))
    tiles = [jnp.zeros((64, 128), F32) for _ in range(3)]
    for j, (offset, count) in enumerate(block_slots(counts, block * 4)):
        freq = block * 4 + j
        rows = [spectrum[pl.ds(pl.multiple_of((c * 128 + freq) * 32, 32), 32), :] for c in range(2)]
        coeffs = jnp.dot(
            jnp.concatenate(rows, 0).astype(BF16), basis[freq], preferred_element_type=F32
        )
        turned = pltpu.roll(coeffs, offset % 128, 1)
        tiles = [
            jnp.where(slot_mask(lane, t, offset, count), turned, tiles[t]) for t in range(3)
        ]
    fold_slots(*tiles, out.at[block])


def fold_slots(low, middle, high, out):
    out[0:64] = low.astype(BF16)
    out[64:128] = middle.astype(BF16)
    lane = lanes((32, 128))
    out[128:160] = jnp.where(lane < 64, high[0:32], pltpu.roll(high[32:64], 64, 1)).astype(BF16)


def unfold_slots(high):
    lane = lanes((32, 128))
    high = high.astype(F32)
    first = jnp.where(lane < 64, high, 0.0)
    second = jnp.where(lane < 64, pltpu.roll(high, 64, 1), 0.0)
    return jnp.concatenate([first, second], 0)


def pick_slots(tiles, lane, offset, count):
    picked = jnp.zeros_like(tiles[0])
    for t in range(3):
        picked = jnp.where(slot_mask(lane, t, offset, count), tiles[t], picked)
    return pltpu.roll(picked, (128 - offset % 128) % 128, 1)


def unpack_block(counts, packed, basis, block, out):
    lane = lanes((64, 128))
    tiles = [
        packed[block, 0:64].astype(F32),
        packed[block, 64:128].astype(F32),
        unfold_slots(packed[block, 128:160]),
    ]
    for j, (offset, count) in enumerate(block_slots(counts, block * 4)):
        freq = block * 4 + j
        cleaned = pick_slots(tiles, lane, offset, count).astype(BF16)
        back = lax.dot_general(
            cleaned, basis[freq], (((1,), (1,)), ((), ())), preferred_element_type=F32
        ).astype(BF16)
        for c in range(2):
            out[c * 128 + freq] = back[c * 32 : c * 32 + 32]


def chunk_slots(packed, sources):
    rows = [packed[s] for s in sources]
    low = jnp.concatenate([r[0:64] for r in rows], 0).astype(F32)
    middle = jnp.concatenate([r[64:128] for r in rows], 0).astype(F32)
    high = jnp.concatenate([unfold_slots(r[128:160]) for r in rows], 0)
    return low, middle, high


def store_groups(all_ids, groups, sources):
    rows = jnp.concatenate([all_ids[s] for s in sources], 0).astype(F32)
    rows = jnp.concatenate([rows, jnp.zeros((4, 96), F32)], 1)
    turned = jnp.concatenate([rows, jnp.zeros((124, 128), F32)], 0).T[0:32]
    for i, s in enumerate(sources):
        groups[s] = jnp.broadcast_to(turned[:, i : i + 1], (32, 128))


def chunk_groups(groups, sources):
    return jnp.concatenate([r for s in sources for r in [groups[s]] * 2], 0)


def make_tables(slots, gains, first_freq, gram, table, member):
    gram[...] = jnp.zeros_like(gram)
    row = lax.broadcasted_iota(jnp.int32, (8, 512), 0)
    lane = lanes((8, 512))
    slot_gain = jnp.zeros((8, 512), F32)
    for j, (offset, count) in enumerate(slots):
        column = jnp.zeros((8, 512), F32)
        for g in range(8):
            column = jnp.where(row == g, gains[g, first_freq + j], column)
        here = ((lane >= offset) & (lane < offset + count)) | (lane == 384 + j)
        slot_gain = jnp.where(here, column, slot_gain)
    high = slot_gain.astype(BF16).astype(F32)
    middle = (slot_gain - high).astype(BF16).astype(F32)
    low = slot_gain - high - middle
    table[...] = jnp.concatenate([high, middle, low, jnp.zeros((104, 512), F32)], 0).astype(BF16)
    row = lax.broadcasted_iota(jnp.int32, (384, 128), 0)
    lane = lanes((384, 128))
    inside = jnp.zeros((384, 128), F32)
    for j, (offset, count) in enumerate(slots):
        inside = jnp.where((lane == j) & (row >= offset) & (row < offset + count), 1.0, inside)
    member[...] = inside.astype(BF16)


def add_chunk(packed, groups, sources, gram, table, member, sums):
    fourth, total = sums
    lane = lanes((256, 128))
    wanted = jnp.where(lane < 24, lane % 8, -1).astype(F32)
    value = jnp.concatenate(chunk_slots(packed, sources), 1)
    onehot = jnp.where(chunk_groups(groups, sources) == wanted, 1.0, 0.0).astype(BF16)
    gain = jnp.dot(onehot, table[...], preferred_element_type=F32)
    scaled = (value * gain[:, 0:384]).astype(BF16)
    products = lax.dot_general(
        scaled, scaled, (((0,), (0,)), ((), ())), preferred_element_type=F32
    )
    for t in range(3):
        gram[t, 0:384] += products[:, t * 128 : t * 128 + 128]
    square = value * value
    upper = square.astype(BF16)
    lower = (square - upper.astype(F32)).astype(BF16)
    norms = jnp.dot(upper, member[...], preferred_element_type=F32)
    norms += jnp.dot(lower, member[...], preferred_element_type=F32)
    weight = gain[:, 384:512] * gain[:, 384:512]
    fourth += jnp.sum(weight * norms * norms, 0, keepdims=True)
    total += jnp.sum(weight, 0, keepdims=True)
    return fourth, total


def gather_grams(slots, gram, sums, out):
    fourth, total = sums
    row = lax.broadcasted_iota(jnp.int32, (128, 128), 0)
    lane = lanes((128, 128))
    squares = []
    for offset, count in slots:
        tiles = [gram[t, pl.ds(offset, 128)] for t in range(3)]
        squares.append(jnp.where(row < count, pick_slots(tiles, lane, offset, count), 0.0))
    for half in range(2):
        upper, lower = squares[half * 2], squares[half * 2 + 1]
        out[half, 0:128] = jnp.where(row <= lane, upper, lower)
        diagonal = jnp.sum(jnp.where(row == lane, lower, 0.0), 0, keepdims=True)
        out[half, 128:136] = jnp.concatenate(
            [diagonal, fourth, total, jnp.zeros((5, 128), F32)], 0
        )


def split(value):
    high = value.astype(BF16)
    return high, (value - high.astype(F32)).astype(BF16)


def right_side(value):
    high, low = split(value)
    return jnp.concatenate(
        [jnp.concatenate([high, low], 1), jnp.concatenate([high, jnp.zeros_like(high)], 1)], 0
    )


def product(left, right):
    high, low = split(left)
    wide = jnp.dot(jnp.concatenate([high, low], 1), right, preferred_element_type=F32)
    return wide[:, 0:128] + wide[:, 128:256]


def total_of(value):
    return jnp.sum(jnp.sum(value, 0, keepdims=True), 1, keepdims=True)


def main_kernel(
    image_total, counts_in, gains_in, noise_in, images, basis_in, forward_in, ids_in, out,
    counts, gains, noise, forward, my_ids, pixels, spectrum, basis, packed, arrived, cleaned, returned, all_ids, groups, gram, table, member,
    part, other, mine, parts, cov_ref, cov_right, size, trace,
    my_filters, other_filters, shifted, filters,
    local, load, load_basis, load_small, send, recv, send_ids, recv_ids, send_back, recv_back, send_sum, recv_sum,
):
    x, y, z, core = place()
    me = owner_index(x, y, z)
    quarter, low = z // 2, z % 2
    smalls = [(counts_in, counts), (gains_in, gains), (noise_in, noise)]
    smalls += [(forward_in, forward), (ids_in, my_ids)]
    smalls = [
        pltpu.make_async_copy(source, target, load_small.at[i])
        for i, (source, target) in enumerate(smalls)
    ]
    for copy in smalls:
        copy.start()

    def image_copy(m):
        rows = pl.ds(pl.multiple_of(m * 512, 512), 512)
        return pltpu.make_async_copy(images.at[rows], pixels.at[rows], load.at[m])

    def basis_copy(m):
        freqs = pl.ds(m * 32, 32)
        return pltpu.make_async_copy(basis_in.at[freqs], basis.at[freqs], load_basis.at[m])

    for m in range(8):
        image_copy(m).start()
    for m in range(4):
        basis_copy(m).start()
    partner = {"img": y * 8 + z, "grp": x * 2 + 1 - core}
    column = []
    for step in (2, 1, 3):
        column.append({"img": y * 8 + (quarter + step) % 4 * 2 + low, "grp": x * 2 + core})
    barrier = pltpu.get_barrier_semaphore()
    for device in [peer_of(i, 1)[0] for i in range(31)] + [partner] + column:
        pl.semaphore_signal(barrier, inc=1, device_id=device, device_id_type=MESH_ID)
    for copy in smalls:
        copy.wait()
    slots = block_slots(counts, me * 4)

    def remote(source, target, sent, received, device):
        return pltpu.make_async_remote_copy(
            source, target, sent, received, device_id=device, device_id_type=MESH_ID
        )

    def data_copy(i):
        device, index = peer_of(i, 1)
        return remote(packed.at[index], arrived.at[me], send.at[i], recv.at[i], device)

    def ids_copy(i):
        return remote(my_ids, all_ids.at[me], send_ids.at[i], recv_ids.at[i], peer_of(i, 1)[0])

    def back_copy(i):
        device, index = peer_of(i, 1)
        return remote(cleaned.at[index], returned.at[me], send_back.at[i], recv_back.at[i], device)

    def sum_copy(source, target, i, device):
        return remote(source, target, send_sum.at[i], recv_sum.at[i], device)

    @pl.loop(0, 8)
    def _(m):
        image_copy(m).wait()
        rows = pl.ds(pl.multiple_of(m * 512, 512), 512)
        lines = lax.dot_general(
            forward[...], pixels[rows, :], (((1,), (1,)), ((), ())), preferred_element_type=F32
        )
        for n in range(4):
            spectrum[pl.ds(m * 4 + n, 256, stride=32), :] = lines[:, n * 128 : n * 128 + 128]

    pl.semaphore_wait(barrier, 35)

    for m in range(4):
        basis_copy(m).wait()

    def send_block(i):
        ids_copy(i).start()
        data_copy(i).start()

    @pl.loop(0, 16)
    def _(pair):
        for half in range(2):
            pack_block(counts, spectrum, basis, peer_of(pair * 2 + half, 1)[1], packed)

        send_block(pair * 2)

        @pl.when(pair < 15)
        def _():
            send_block(pair * 2 + 1)

    own = pltpu.make_async_copy(packed.at[me], arrived.at[me], local.at[0])
    own.start()
    own_ids = pltpu.make_async_copy(my_ids, all_ids.at[me], local.at[1])
    own_ids.start()
    make_tables(slots, gains, me * 4, gram, table, member)
    own_ids.wait()
    own.wait()

    def chunk(m, sums):
        sources = []
        for s in range(4):
            i = m * 4 + s
            if s < 3:
                data_copy(i).wait_recv()
                ids_copy(i).wait_recv()
            else:

                @pl.when(i < 31)
                def _():
                    data_copy(i).wait_recv()
                    ids_copy(i).wait_recv()

            sources.append(peer_of(i, -1)[1])
        store_groups(all_ids, groups, sources)
        return add_chunk(arrived, groups, sources, gram, table, member, sums)

    nothing = jnp.zeros((1, 128), F32)
    gather_grams(slots, gram, lax.fori_loop(0, 8, chunk, (nothing, nothing)), part)

    swap = sum_copy(part.at[1 - core], other, 0, partner)
    swap.start()
    swap.wait()
    both = part[core] + other[...]
    mine[...] = both
    copies = [sum_copy(mine, parts.at[quarter], i + 1, d) for i, d in enumerate(column)]
    for copy in copies:
        copy.start()
    parts[quarter] = both
    shifted[...] = jnp.zeros_like(shifted)

    @pl.loop(0, 31)
    def _(i):
        ids_copy(i).wait_send()
        data_copy(i).wait_send()

    for copy in copies:
        copy.wait()
    make_covariances(image_total, counts, parts, cov_ref, cov_right, size, trace)

    def send_pair(pair):
        groups = pl.ds(pair * 2, 2)
        return sum_copy(my_filters.at[groups], other_filters.at[groups], pair + 4, partner)

    def place_pair(pair):
        for half in range(2):
            place_filters(slots, pair * 2 + half, my_filters, other_filters, shifted, filters)

    @pl.loop(0, 4)
    def _(pair):
        make_filters(pair, gains, noise, my_filters, cov_ref, cov_right, size, trace)
        send_pair(pair).start()

    @pl.loop(0, 4)
    def _(pair):
        send_pair(pair).wait()
        place_pair(pair)

    @pl.loop(0, 8)
    def _(m):
        apply_chunk(arrived, groups, [peer_of(m * 4 + s, 1)[1] for s in range(4)], filters, cleaned)
        for s in range(4):
            i = m * 4 + s
            if s < 3:
                back_copy(i).start()
            else:

                @pl.when(i < 31)
                def _():
                    back_copy(i).start()

    unpack_block(counts, cleaned, basis, me, out)

    @pl.loop(0, 15)
    def _(pair):
        for half in range(2):
            back_copy(pair * 2 + half).wait()
        for half in range(2):
            unpack_block(counts, returned, basis, peer_of(pair * 2 + half, -1)[1], out)

    back_copy(30).wait()
    unpack_block(counts, returned, basis, peer_of(30, -1)[1], out)


def make_covariances(images, counts, parts, cov_ref, cov_right, size, trace):
    x, y, z, core = place()
    first_freq = owner_index(x, y, z) * 4 + core * 2
    row = lax.broadcasted_iota(jnp.int32, (128, 128), 0)
    lane = lanes((128, 128))
    line = lanes((1, 128))
    block = ((parts[0] + parts[1]) + parts[2]) + parts[3]
    square = block[0:128]
    above = jnp.where(row < lane, square, 0.0)
    below = jnp.where(row > lane, square, 0.0)
    grams = (
        jnp.where(row <= lane, square, 0.0) + above.T,
        jnp.where(row == lane, block[128:129], below) + below.T,
    )
    for j in range(2):
        count = counts[first_freq + j]
        here = line == core * 2 + j
        fourth = jnp.sum(jnp.where(here, block[129:130], 0.0), 1, keepdims=True)
        total = jnp.sum(jnp.where(here, block[130:131], 0.0), 1, keepdims=True)
        sample = grams[j] / total
        ident = jnp.where((row == lane) & (row < count), 1.0, 0.0)
        level = total_of(sample * ident) / count.astype(F32)
        off_level = sample - level * ident
        spread = total_of(off_level * off_level)
        excess = (fourth / total - total_of(sample * sample)) / (2.0 * images)
        weight = excess / (excess + spread)
        cov = (1.0 - weight) * sample + (weight * level) * ident
        right = right_side(cov)
        square = product(cov, right)
        cov_ref[j, 0] = cov
        cov_ref[j, 1] = square
        cov_ref[j, 2] = product(square, right)
        cov_right[j] = right
        size[j] = jnp.broadcast_to(total_of(cov * cov), (8, 128))
        trace[j] = jnp.broadcast_to(total_of(cov * ident), (8, 128))


def make_filters(pair, gains, noise, out, cov_ref, cov_right, size, trace):
    x, y, z, core = place()
    first_freq = owner_index(x, y, z) * 4 + core * 2
    ident = jnp.where(
        lax.broadcasted_iota(jnp.int32, (128, 128), 0) == lanes((128, 128)), 1.0, 0.0
    )
    problems = [(pair * 2 + g, j) for g in range(2) for j in range(2)]
    powers, sums, scales = [], [], []
    for g, j in problems:
        gain, level = gains[g, first_freq + j], noise[first_freq + j]
        square = gain * gain
        norm = size[j, 0:1, 0:1] * (square * square)
        norm += trace[j, 0:1, 0:1] * (2.0 * square * level) + 128.0 * level * level
        scale = 1.0 / jnp.sqrt(norm)
        keep, slope = 1.0 - scale * level, scale * square
        first, second, third = cov_ref[j, 0], cov_ref[j, 1], cov_ref[j, 2]
        power = keep * ident - slope * first
        twice = keep * keep * ident - (2.0 * keep * slope) * first + slope * slope * second
        thrice = (
            keep * keep * keep * ident - (3.0 * keep * keep * slope) * first
            + (3.0 * keep * slope * slope) * second - slope * slope * slope * third
        )
        powers.append(twice)
        sums.append(ident + power + twice + thrice)
        scales.append(scale * gain)
    powers = [product(p, right_side(p)) for p in powers]
    for _ in range(NS_ITERS - 3):
        sides = [right_side(p) for p in powers]
        both = [product(jnp.concatenate([s, p], 0), r) for s, p, r in zip(sums, powers, sides)]
        sums = [s + b[0:128] for s, b in zip(sums, both)]
        powers = [b[128:256] for b in both]
    sums = [s + product(s, right_side(p)) for s, p in zip(sums, powers)]
    for (g, j), s, scale in zip(problems, sums, scales):
        out[g, j] = (scale * product(s, cov_right[j])).astype(BF16)


def place_filters(slots, g, mine, other, shifted, filters):
    core = place()[3]
    lane = lanes((128, 128))
    tiles = [[jnp.zeros((128, 128), F32)] * 3 for _ in range(3)]
    for j, (offset, count) in enumerate(slots):
        value = jnp.where(core == j // 2, mine[g, j % 2].astype(F32), other[g, j % 2].astype(F32))
        shifted[j, 128:256] = pltpu.roll(value, offset % 128, 1)
        for r in range(3):
            start = jnp.clip(r * 128 + 128 - offset, 0, 256)
            rows = shifted[j, pl.ds(start, 128)]
            for t in range(3):
                tiles[r][t] += jnp.where(slot_mask(lane, t, offset, count), rows, 0.0)
    for r in range(3):
        row = pl.ds(pl.multiple_of(g * 384 + r * 128, 128), 128)
        for t in range(3):
            filters[row, t * 128 : t * 128 + 128] = tiles[r][t].astype(BF16)


def apply_chunk(packed, groups, sources, filters, out):
    value = jnp.concatenate(chunk_slots(packed, sources), 1).astype(BF16)
    group = chunk_groups(groups, sources)
    pieces = []
    for g in range(8):
        mask = jnp.where(group == float(g), 1.0, 0.0).astype(BF16)
        pieces.append(value * jnp.concatenate([mask] * 3, 1))
    cleaned = jnp.dot(jnp.concatenate(pieces, 1), filters[...], preferred_element_type=F32)
    for s, source in enumerate(sources):
        rows = cleaned[s * 64 : s * 64 + 64]
        fold_slots(rows[:, 0:128], rows[:, 128:256], rows[:, 256:384], out.at[source])


def dft_tables(angles, freqs):
    angle_index, freq_index = np.arange(angles), np.arange(freqs)
    turns = angle_index[:, None] * freq_index[None, :] % angles
    phases = turns.astype(np.float32) * np.float32(2.0 * math.pi / angles)
    factor = np.float32(1.0 / math.sqrt(angles))
    cosine = np.cos(phases) * factor
    sine = -np.sin(phases) * factor
    doubling = np.where(freq_index == 0, 1.0, 2.0).astype(np.float32)
    forward = np.concatenate([cosine, sine], 1).T
    inverse = np.concatenate([cosine * doubling, sine * doubling], 1).T
    return forward.astype(BF16), inverse.astype(BF16)


def body(images, group_ids, counts, radial_basis, ctf_gain, noise_var):
    local_images, radii, angles = images.shape
    freqs = radial_basis.shape[0]
    image_total = local_images * lax.axis_size("img") * lax.axis_size("grp")
    dma = pltpu.SemaphoreType.DMA
    forward, inverse = dft_tables(angles, freqs)
    ids = group_ids.reshape(1, local_images)
    data = pltpu.VMEM((32, 160, 128), BF16)
    sums = pltpu.VMEM((136, 128), F32)
    pairs = pltpu.VMEM((8, 2, 128, 128), BF16)
    small = pltpu.VMEM((2, 8, 128), F32)
    hbm = pl.BlockSpec(memory_space=pltpu.HBM)
    back = pl.pallas_call(
        functools.partial(main_kernel, image_total),
        out_shape=jax.ShapeDtypeStruct((2 * freqs, local_images, radii), BF16),
        in_specs=[hbm] * 7,
        out_specs=VMEM,
        scratch_shapes=[
            pltpu.SMEM(counts.shape, jnp.int32), pltpu.SMEM(ctf_gain.shape, F32),
            pltpu.SMEM(noise_var.shape, F32), pltpu.VMEM(forward.shape, BF16),
            pltpu.VMEM(ids.shape, jnp.int32),
            pltpu.VMEM((local_images * radii, angles), BF16),
            pltpu.VMEM((2 * freqs * local_images, radii), F32),
            pltpu.VMEM(radial_basis.shape, BF16),
            data, data, data, data,
            pltpu.VMEM((32, 1, 32), jnp.int32), pltpu.VMEM((32, 32, 128), F32),
            pltpu.VMEM((3, 512, 128), F32), pltpu.VMEM((128, 512), BF16),
            pltpu.VMEM((384, 128), BF16),
            pltpu.VMEM((2, 136, 128), F32), sums, sums, pltpu.VMEM((4, 136, 128), F32),
            pltpu.VMEM((2, 3, 128, 128), F32), pltpu.VMEM((2, 256, 256), BF16), small, small,
            pairs, pairs, pltpu.VMEM((4, 384, 128), F32), pltpu.VMEM((3072, 384), BF16),
            dma((2,)), dma((8,)), dma((4,)), dma((5,)),
            dma((31,)), dma((31,)), dma((31,)), dma((31,)), dma((31,)), dma((31,)),
            dma((8,)), dma((8,)),
        ],
        compiler_params=pltpu.CompilerParams(collective_id=0, has_side_effects=True),
        name="denoise",
    )(
        counts, ctf_gain, noise_var, images.reshape(local_images * radii, angles), radial_basis,
        jnp.asarray(forward), ids,
    )
    denoised = jnp.einsum("knr,ka->nra", back, jnp.asarray(inverse), preferred_element_type=F32)
    return denoised.astype(BF16)


def solution(mesh):
    placed = (P(("img", "grp"), None, None), P(("img", "grp")), P(), P(), P(), P())
    return jax.shard_map(
        body, mesh=mesh, in_specs=placed, out_specs=P(("img", "grp"), None, None), check_vma=False
    )
```

```python
import functools
import math

import jax
import jax.numpy as jnp
import numpy as np
from jax import lax
from jax.experimental import pallas as pl
from jax.experimental.pallas import tpu as pltpu
from jax.sharding import PartitionSpec as P

NS_ITERS = 7
SIDE = 4
MESH_ID = pl.DeviceIdType.MESH
F32 = jnp.float32
BF16 = jnp.bfloat16


def rem(a, n):
    return a % n if isinstance(a, int) else lax.rem(a, jnp.int32(n))


def div(a, n):
    return a // n if isinstance(a, int) else lax.div(a, jnp.int32(n))


def place():
    img = lax.axis_index("img")
    grp = lax.axis_index("grp")
    return div(grp, 2), div(img, 8), rem(img, 8), rem(grp, 2)


def owner_index(x, y, z):
    return x * 8 + y * 2 + rem(z, 2)


def step_of(i):
    turn = rem(i, 4)
    return rem(turn + 1, 4), rem(div(i, 4) + turn + 2, 4), 1 - div(i, 16)


def peer_of(i, sign):
    x, y, z, core = place()
    a, b, c = step_of(i)
    px, py = rem(x + SIDE + sign * a, SIDE), rem(y + SIDE + sign * b, SIDE)
    pz = div(z, 2) * 2 + rem(z + c, 2)
    return {"img": py * 8 + pz, "grp": px * 2 + core}, owner_index(px, py, pz)


def lanes(shape):
    return lax.broadcasted_iota(jnp.int32, shape, len(shape) - 1)


def tile(index):
    return pl.ds(pl.multiple_of(index * 128, 128), 128)


def block_slots(counts, first):
    offsets, offset = [], 0
    for j in range(4):
        count = counts[first + j]
        offsets.append((offset, count))
        offset = offset + count
    return offsets


def slot_mask(lane, t, offset, count):
    slot = lane + t * 128
    return (slot >= offset) & (slot < offset + count)


def pack_block(counts, spectrum, basis, block, out):
    lane = lanes((64, 128))
    tiles = [jnp.zeros((64, 128), F32) for _ in range(3)]
    for j, (offset, count) in enumerate(block_slots(counts, block * 4)):
        freq = block * 4 + j
        rows = [spectrum[pl.ds(pl.multiple_of((c * 128 + freq) * 32, 32), 32), :] for c in range(2)]
        coeffs = jnp.dot(
            jnp.concatenate(rows, 0).astype(BF16), basis[freq], preferred_element_type=F32
        )
        turned = pltpu.roll(coeffs, offset % 128, 1)
        tiles = [
            jnp.where(slot_mask(lane, t, offset, count), turned, tiles[t]) for t in range(3)
        ]
    fold_slots(*tiles, out.at[block])


def fold_slots(low, middle, high, out):
    out[0:64] = low.astype(BF16)
    out[64:128] = middle.astype(BF16)
    lane = lanes((32, 128))
    out[128:160] = jnp.where(lane < 64, high[0:32], pltpu.roll(high[32:64], 64, 1)).astype(BF16)


def unfold_slots(high):
    lane = lanes((32, 128))
    high = high.astype(F32)
    first = jnp.where(lane < 64, high, 0.0)
    second = jnp.where(lane < 64, pltpu.roll(high, 64, 1), 0.0)
    return jnp.concatenate([first, second], 0)


def pick_slots(tiles, lane, offset, count):
    picked = jnp.zeros_like(tiles[0])
    for t in range(3):
        picked = jnp.where(slot_mask(lane, t, offset, count), tiles[t], picked)
    return pltpu.roll(picked, (128 - offset % 128) % 128, 1)


def unpack_block(counts, packed, basis, block, out, out_hbm, sent):
    lane = lanes((64, 128))
    tiles = [
        packed[block, 0:64].astype(F32),
        packed[block, 64:128].astype(F32),
        unfold_slots(packed[block, 128:160]),
    ]
    for j, (offset, count) in enumerate(block_slots(counts, block * 4)):
        freq = block * 4 + j
        cleaned = pick_slots(tiles, lane, offset, count).astype(BF16)
        back = lax.dot_general(
            cleaned, basis[freq], (((1,), (1,)), ((), ())), preferred_element_type=F32
        ).astype(BF16)
        for c in range(2):
            out[c * 128 + freq] = back[c * 32 : c * 32 + 32]
    for c in range(2):
        rows = pl.ds(c * 128 + block * 4, 4)
        pltpu.make_async_copy(out.at[rows], out_hbm.at[rows], sent).start()


def chunk_slots(packed, sources):
    rows = [packed[s] for s in sources]
    low = jnp.concatenate([r[0:64] for r in rows], 0).astype(F32)
    middle = jnp.concatenate([r[64:128] for r in rows], 0).astype(F32)
    high = jnp.concatenate([unfold_slots(r[128:160]) for r in rows], 0)
    return low, middle, high


def store_groups(all_ids, groups, sources):
    rows = jnp.concatenate([all_ids[s] for s in sources], 0).astype(F32)
    rows = jnp.concatenate([rows, jnp.zeros((4, 96), F32)], 1)
    turned = jnp.concatenate([rows, jnp.zeros((124, 128), F32)], 0).T[0:32]
    for i, s in enumerate(sources):
        groups[s] = jnp.broadcast_to(turned[:, i : i + 1], (32, 128))


def chunk_groups(groups, sources):
    return jnp.concatenate([r for s in sources for r in [groups[s]] * 2], 0)


def make_tables(slots, gains, first_freq, gram, table, member):
    gram[...] = jnp.zeros_like(gram)
    row = lax.broadcasted_iota(jnp.int32, (8, 512), 0)
    lane = lanes((8, 512))
    slot_gain = jnp.zeros((8, 512), F32)
    for j, (offset, count) in enumerate(slots):
        column = jnp.zeros((8, 512), F32)
        for g in range(8):
            column = jnp.where(row == g, gains[g, first_freq + j], column)
        here = ((lane >= offset) & (lane < offset + count)) | (lane == 384 + j)
        slot_gain = jnp.where(here, column, slot_gain)
    high = slot_gain.astype(BF16).astype(F32)
    middle = (slot_gain - high).astype(BF16).astype(F32)
    low = slot_gain - high - middle
    table[...] = jnp.concatenate([high, middle, low, jnp.zeros((104, 512), F32)], 0).astype(BF16)
    row = lax.broadcasted_iota(jnp.int32, (384, 128), 0)
    lane = lanes((384, 128))
    inside = jnp.zeros((384, 128), F32)
    for j, (offset, count) in enumerate(slots):
        inside = jnp.where((lane == j) & (row >= offset) & (row < offset + count), 1.0, inside)
    member[...] = inside.astype(BF16)


def add_chunk(packed, groups, sources, gram, table, member, sums):
    fourth, total = sums
    lane = lanes((256, 128))
    wanted = jnp.where(lane < 24, lane % 8, -1).astype(F32)
    value = jnp.concatenate(chunk_slots(packed, sources), 1)
    onehot = jnp.where(chunk_groups(groups, sources) == wanted, 1.0, 0.0).astype(BF16)
    gain = jnp.dot(onehot, table[...], preferred_element_type=F32)
    scaled = (value * gain[:, 0:384]).astype(BF16)
    products = lax.dot_general(
        scaled, scaled, (((0,), (0,)), ((), ())), preferred_element_type=F32
    )
    for t in range(3):
        gram[t, 0:384] += products[:, t * 128 : t * 128 + 128]
    square = value * value
    upper = square.astype(BF16)
    lower = (square - upper.astype(F32)).astype(BF16)
    norms = jnp.dot(upper, member[...], preferred_element_type=F32)
    norms += jnp.dot(lower, member[...], preferred_element_type=F32)
    weight = gain[:, 384:512] * gain[:, 384:512]
    fourth += jnp.sum(weight * norms * norms, 0, keepdims=True)
    total += jnp.sum(weight, 0, keepdims=True)
    return fourth, total


def gather_grams(slots, gram, sums, out):
    fourth, total = sums
    row = lax.broadcasted_iota(jnp.int32, (128, 128), 0)
    lane = lanes((128, 128))
    squares = []
    for offset, count in slots:
        tiles = [gram[t, pl.ds(offset, 128)] for t in range(3)]
        squares.append(jnp.where(row < count, pick_slots(tiles, lane, offset, count), 0.0))
    for half in range(2):
        upper, lower = squares[half * 2], squares[half * 2 + 1]
        out[half, 0:128] = jnp.where(row <= lane, upper, lower)
        diagonal = jnp.sum(jnp.where(row == lane, lower, 0.0), 0, keepdims=True)
        out[half, 128:136] = jnp.concatenate(
            [diagonal, fourth, total, jnp.zeros((5, 128), F32)], 0
        )


def split(value):
    high = value.astype(BF16)
    return high, (value - high.astype(F32)).astype(BF16)


def right_side(value):
    high, low = split(value)
    return jnp.concatenate(
        [jnp.concatenate([high, low], 1), jnp.concatenate([high, jnp.zeros_like(high)], 1)], 0
    )


def product(left, right):
    high, low = split(left)
    wide = jnp.dot(jnp.concatenate([high, low], 1), right, preferred_element_type=F32)
    return wide[:, 0:128] + wide[:, 128:256]


def total_of(value):
    return jnp.sum(jnp.sum(value, 0, keepdims=True), 1, keepdims=True)


def main_kernel(
    image_total, counts_in, gains_in, noise_in, images, basis_in, forward_in, ids_in, out_hbm,
    out, counts, gains, noise, forward, my_ids, pixels, spectrum, basis, packed, arrived, cleaned, returned, all_ids, groups, gram, table, member,
    part, other, mine, parts, cov_ref, cov_right, size, trace,
    my_filters, other_filters, shifted, filters, filters_last,
    local, load, load_basis, load_small, send, recv, send_ids, recv_ids, send_back, recv_back, send_sum, recv_sum,
):
    x, y, z, core = place()
    me = owner_index(x, y, z)
    quarter, low = z // 2, z % 2
    smalls = [(counts_in, counts), (gains_in, gains), (noise_in, noise)]
    smalls += [(forward_in, forward), (ids_in, my_ids)]
    smalls = [
        pltpu.make_async_copy(source, target, load_small.at[i])
        for i, (source, target) in enumerate(smalls)
    ]
    for copy in smalls:
        copy.start()

    def image_copy(m):
        rows = pl.ds(pl.multiple_of(m * 1024, 1024), 1024)
        return pltpu.make_async_copy(images.at[rows], pixels.at[rows], load.at[m])

    def basis_copy(m):
        freqs = pl.ds(m * 32, 32)
        return pltpu.make_async_copy(basis_in.at[freqs], basis.at[freqs], load_basis.at[m])

    for m in range(4):
        image_copy(m).start()
    for m in range(4):
        basis_copy(m).start()
    partner = {"img": y * 8 + z, "grp": x * 2 + 1 - core}
    column = []
    for step in (2, 1, 3):
        column.append({"img": y * 8 + (quarter + step) % 4 * 2 + low, "grp": x * 2 + core})
    barrier = pltpu.get_barrier_semaphore()
    for device in [peer_of(i, 1)[0] for i in range(31)] + [partner] + column:
        pl.semaphore_signal(barrier, inc=1, device_id=device, device_id_type=MESH_ID)
    for copy in smalls:
        copy.wait()
    slots = block_slots(counts, me * 4)

    def remote(source, target, sent, received, device):
        return pltpu.make_async_remote_copy(
            source, target, sent, received, device_id=device, device_id_type=MESH_ID
        )

    def data_copy(i):
        device, index = peer_of(i, 1)
        return remote(packed.at[index], arrived.at[me], send.at[i], recv.at[i], device)

    def ids_copy(i):
        return remote(my_ids, all_ids.at[me], send_ids.at[i], recv_ids.at[i], peer_of(i, 1)[0])

    def back_copy(i):
        device, index = peer_of(i, 1)
        return remote(cleaned.at[index], returned.at[me], send_back.at[i], recv_back.at[i], device)

    def sum_copy(source, target, i, device):
        return remote(source, target, send_sum.at[i], recv_sum.at[i], device)

    @pl.loop(0, 4)
    def _(m):
        image_copy(m).wait()
        rows = pl.ds(pl.multiple_of(m * 1024, 1024), 1024)
        lines = lax.dot_general(
            forward[...], pixels[rows, :], (((1,), (1,)), ((), ())), preferred_element_type=F32
        )
        for n in range(8):
            spectrum[pl.ds(m * 8 + n, 256, stride=32), :] = lines[:, n * 128 : n * 128 + 128]

    pl.semaphore_wait(barrier, 35)

    for m in range(4):
        basis_copy(m).wait()

    def send_block(i):
        ids_copy(i).start()
        data_copy(i).start()

    @pl.loop(0, 16)
    def _(pair):
        for half in range(2):
            pack_block(counts, spectrum, basis, peer_of(pair * 2 + half, 1)[1], packed)

        send_block(pair * 2)

        @pl.when(pair < 15)
        def _():
            send_block(pair * 2 + 1)

    own = pltpu.make_async_copy(packed.at[me], arrived.at[me], local.at[0])
    own.start()
    own_ids = pltpu.make_async_copy(my_ids, all_ids.at[me], local.at[1])
    own_ids.start()
    make_tables(slots, gains, me * 4, gram, table, member)
    own_ids.wait()
    own.wait()

    def chunk(m, sums):
        sources = []
        for s in range(4):
            i = m * 4 + s
            if s < 3:
                data_copy(i).wait_recv()
                ids_copy(i).wait_recv()
            else:

                @pl.when(i < 31)
                def _():
                    data_copy(i).wait_recv()
                    ids_copy(i).wait_recv()

            sources.append(peer_of(i, -1)[1])
        store_groups(all_ids, groups, sources)
        return add_chunk(arrived, groups, sources, gram, table, member, sums)

    nothing = jnp.zeros((1, 128), F32)
    gather_grams(slots, gram, lax.fori_loop(0, 8, chunk, (nothing, nothing)), part)

    swap = sum_copy(part.at[1 - core], other, 0, partner)
    swap.start()
    swap.wait()
    both = part[core] + other[...]
    mine[...] = both
    copies = [sum_copy(mine, parts.at[quarter], i + 1, d) for i, d in enumerate(column)]
    for copy in copies:
        copy.start()
    parts[quarter] = both
    shifted[...] = jnp.zeros_like(shifted)

    @pl.loop(0, 31)
    def _(i):
        ids_copy(i).wait_send()
        data_copy(i).wait_send()

    for copy in copies:
        copy.wait()
    make_covariances(image_total, counts, parts, cov_ref, cov_right, size, trace)

    def send_pair(pair):
        groups = pl.ds(pair * 2, 2)
        return sum_copy(my_filters.at[groups], other_filters.at[groups], pair + 4, partner)

    def place_pair(pair):
        for half in range(2):
            place_filters(
                slots, pair, half, my_filters, other_filters, shifted, filters, filters_last
            )

    @pl.loop(0, 2)
    def _(half):
        make_filters(half, gains, noise, my_filters, cov_ref, cov_right, size, trace)
        for pair in range(2):
            send_pair(half * 2 + pair).start()

    @pl.loop(0, 4)
    def _(pair):
        send_pair(pair).wait()
        place_pair(pair)

    @pl.loop(0, 8)
    def _(m):
        sources = [peer_of(m * 4 + s, 1)[1] for s in range(4)]
        apply_chunk(arrived, groups, sources, filters, filters_last, cleaned)
        for s in range(4):
            i = m * 4 + s
            if s < 3:
                back_copy(i).start()
            else:

                @pl.when(i < 31)
                def _():
                    back_copy(i).start()

    unpack_block(counts, cleaned, basis, me, out, out_hbm, local.at[2])

    @pl.loop(0, 15)
    def _(pair):
        for half in range(2):
            back_copy(pair * 2 + half).wait()
        for half in range(2):
            index = peer_of(pair * 2 + half, -1)[1]
            unpack_block(counts, returned, basis, index, out, out_hbm, local.at[2])

    back_copy(30).wait()
    unpack_block(counts, returned, basis, peer_of(30, -1)[1], out, out_hbm, local.at[2])
    pltpu.make_async_copy(out, out_hbm, local.at[2]).wait()


def make_covariances(images, counts, parts, cov_ref, cov_right, size, trace):
    x, y, z, core = place()
    first_freq = owner_index(x, y, z) * 4 + core * 2
    row = lax.broadcasted_iota(jnp.int32, (128, 128), 0)
    lane = lanes((128, 128))
    line = lanes((1, 128))
    block = ((parts[0] + parts[1]) + parts[2]) + parts[3]
    square = block[0:128]
    above = jnp.where(row < lane, square, 0.0)
    below = jnp.where(row > lane, square, 0.0)
    grams = (
        jnp.where(row <= lane, square, 0.0) + above.T,
        jnp.where(row == lane, block[128:129], below) + below.T,
    )
    for j in range(2):
        count = counts[first_freq + j]
        here = line == core * 2 + j
        fourth = jnp.sum(jnp.where(here, block[129:130], 0.0), 1, keepdims=True)
        total = jnp.sum(jnp.where(here, block[130:131], 0.0), 1, keepdims=True)
        sample = grams[j] / total
        ident = jnp.where((row == lane) & (row < count), 1.0, 0.0)
        level = total_of(sample * ident) / count.astype(F32)
        off_level = sample - level * ident
        spread = total_of(off_level * off_level)
        excess = (fourth / total - total_of(sample * sample)) / (2.0 * images)
        weight = excess / (excess + spread)
        cov = (1.0 - weight) * sample + (weight * level) * ident
        right = right_side(cov)
        square = product(cov, right)
        cov_ref[j, 0] = cov
        cov_ref[j, 1] = square
        cov_ref[j, 2] = product(square, right)
        cov_right[j] = right
        size[j] = jnp.broadcast_to(total_of(cov * cov), (8, 128))
        trace[j] = jnp.broadcast_to(total_of(cov * ident), (8, 128))


def make_filters(pair, gains, noise, out, cov_ref, cov_right, size, trace):
    x, y, z, core = place()
    first_freq = owner_index(x, y, z) * 4 + core * 2
    ident = jnp.where(
        lax.broadcasted_iota(jnp.int32, (128, 128), 0) == lanes((128, 128)), 1.0, 0.0
    )
    problems = [(pair * 4 + g, j) for g in range(4) for j in range(2)]
    powers, sums, scales = [], [], []
    for g, j in problems:
        gain, level = gains[g, first_freq + j], noise[first_freq + j]
        square = gain * gain
        norm = size[j, 0:1, 0:1] * (square * square)
        norm += trace[j, 0:1, 0:1] * (2.0 * square * level) + 128.0 * level * level
        scale = 1.0 / jnp.sqrt(norm)
        keep, slope = 1.0 - scale * level, scale * square
        first, second, third = cov_ref[j, 0], cov_ref[j, 1], cov_ref[j, 2]
        power = keep * ident - slope * first
        twice = keep * keep * ident - (2.0 * keep * slope) * first + slope * slope * second
        thrice = (
            keep * keep * keep * ident - (3.0 * keep * keep * slope) * first
            + (3.0 * keep * slope * slope) * second - slope * slope * slope * third
        )
        powers.append(twice)
        sums.append(ident + power + twice + thrice)
        scales.append(scale * gain)
    powers = [product(p, right_side(p)) for p in powers]
    for _ in range(NS_ITERS - 3):
        sides = [right_side(p) for p in powers]
        both = [product(jnp.concatenate([s, p], 0), r) for s, p, r in zip(sums, powers, sides)]
        sums = [s + b[0:128] for s, b in zip(sums, both)]
        powers = [b[128:256] for b in both]
    sums = [s + product(s, right_side(p)) for s, p in zip(sums, powers)]
    for (g, j), s, scale in zip(problems, sums, scales):
        out[g, j] = (scale * product(s, cov_right[j])).astype(BF16)


def place_filters(slots, pair, half, mine, other, shifted, filters, filters_last):
    g = pair * 2 + half
    core = place()[3]
    lane = lanes((128, 128))
    tiles = [[jnp.zeros((128, 128), F32)] * 3 for _ in range(3)]
    for j, (offset, count) in enumerate(slots):
        value = jnp.where(core == j // 2, mine[g, j % 2].astype(F32), other[g, j % 2].astype(F32))
        shifted[j, 128:256] = pltpu.roll(value, offset % 128, 1)
        for r in range(3):
            start = jnp.clip(r * 128 + 128 - offset, 0, 256)
            rows = shifted[j, pl.ds(start, 128)]
            for t in range(max(r - 1, 0), min(r + 2, 3)):
                tiles[r][t] = jnp.where(slot_mask(lane, t, offset, count), rows, tiles[r][t])
    for t in range(2):
        column = slice(t * 128, t * 128 + 128)
        for r in range(2):
            row = pl.ds(pl.multiple_of(g * 256 + r * 128, 128), 128)
            filters[row, column] = tiles[r][t].astype(BF16)
        filters[pl.ds(pl.multiple_of(2048 + pair * 128 + half * 64, 64), 64), column] = (
            tiles[2][t][0:64].astype(BF16)
        )
    filters_last[pl.ds(pl.multiple_of(g * 128, 128), 128), :] = tiles[1][2].astype(BF16)
    filters_last[pl.ds(pl.multiple_of(1024 + pair * 128 + half * 64, 64), 64), :] = (
        tiles[2][2][0:64].astype(BF16)
    )


def apply_chunk(packed, groups, sources, filters, filters_last, out):
    low, middle, high = chunk_slots(packed, sources)
    both = jnp.concatenate([low, middle], 1).astype(BF16)
    twice = (high + pltpu.roll(high, 64, 1)).astype(BF16)
    group = chunk_groups(groups, sources)
    second = jnp.where(lanes((256, 128)) >= 64, 1.0, 0.0)
    pieces, ends = [], []
    for g in range(8):
        mask = jnp.where(group == float(g), 1.0, 0.0).astype(BF16)
        pieces.append(both * jnp.concatenate([mask] * 2, 1))
    for pair in range(4):
        mask = jnp.where(group - second == float(pair * 2), 1.0, 0.0).astype(BF16)
        ends.append(twice * mask)
    left = jnp.concatenate(pieces + ends, 1)
    right = jnp.concatenate([p[:, 128:256] for p in pieces] + ends, 1)
    cleaned = jnp.concatenate(
        [
            jnp.dot(left, filters[...], preferred_element_type=F32),
            jnp.dot(right, filters_last[...], preferred_element_type=F32),
        ],
        1,
    )
    for s, source in enumerate(sources):
        rows = cleaned[s * 64 : s * 64 + 64]
        fold_slots(rows[:, 0:128], rows[:, 128:256], rows[:, 256:384], out.at[source])


def dft_tables(angles, freqs):
    angle_index, freq_index = np.arange(angles), np.arange(freqs)
    turns = angle_index[:, None] * freq_index[None, :] % angles
    phases = turns.astype(np.float32) * np.float32(2.0 * math.pi / angles)
    factor = np.float32(1.0 / math.sqrt(angles))
    cosine = np.cos(phases) * factor
    sine = -np.sin(phases) * factor
    doubling = np.where(freq_index == 0, 1.0, 2.0).astype(np.float32)
    forward = np.concatenate([cosine, sine], 1).T
    inverse = np.concatenate([cosine * doubling, sine * doubling], 1).T
    return forward.astype(BF16), inverse.astype(BF16)


def body(images, group_ids, counts, radial_basis, ctf_gain, noise_var):
    local_images, radii, angles = images.shape
    freqs = radial_basis.shape[0]
    image_total = local_images * lax.axis_size("img") * lax.axis_size("grp")
    dma = pltpu.SemaphoreType.DMA
    forward, inverse = dft_tables(angles, freqs)
    ids = group_ids.reshape(1, local_images)
    data = pltpu.VMEM((32, 160, 128), BF16)
    sums = pltpu.VMEM((136, 128), F32)
    pairs = pltpu.VMEM((8, 2, 128, 128), BF16)
    small = pltpu.VMEM((2, 8, 128), F32)
    hbm = pl.BlockSpec(memory_space=pltpu.HBM)
    back = pl.pallas_call(
        functools.partial(main_kernel, image_total),
        out_shape=jax.ShapeDtypeStruct((2 * freqs, local_images, radii), BF16),
        in_specs=[hbm] * 7,
        out_specs=hbm,
        scratch_shapes=[
            pltpu.VMEM((2 * freqs, local_images, radii), BF16),
            pltpu.SMEM(counts.shape, jnp.int32), pltpu.SMEM(ctf_gain.shape, F32),
            pltpu.SMEM(noise_var.shape, F32), pltpu.VMEM(forward.shape, BF16),
            pltpu.VMEM(ids.shape, jnp.int32),
            pltpu.VMEM((local_images * radii, angles), BF16),
            pltpu.VMEM((2 * freqs * local_images, radii), F32),
            pltpu.VMEM(radial_basis.shape, BF16),
            data, data, data, data,
            pltpu.VMEM((32, 1, 32), jnp.int32), pltpu.VMEM((32, 32, 128), F32),
            pltpu.VMEM((3, 512, 128), F32), pltpu.VMEM((128, 512), BF16),
            pltpu.VMEM((384, 128), BF16),
            pltpu.VMEM((2, 136, 128), F32), sums, sums, pltpu.VMEM((4, 136, 128), F32),
            pltpu.VMEM((2, 3, 128, 128), F32), pltpu.VMEM((2, 256, 256), BF16), small, small,
            pairs, pairs, pltpu.VMEM((4, 384, 128), F32), pltpu.VMEM((2560, 256), BF16),
            pltpu.VMEM((1536, 128), BF16),
            dma((3,)), dma((4,)), dma((4,)), dma((5,)),
            dma((31,)), dma((31,)), dma((31,)), dma((31,)), dma((31,)), dma((31,)),
            dma((8,)), dma((8,)),
        ],
        compiler_params=pltpu.CompilerParams(collective_id=0, has_side_effects=True),
        name="denoise",
    )(
        counts, ctf_gain, noise_var, images.reshape(local_images * radii, angles), radial_basis,
        jnp.asarray(forward), ids,
    )
    denoised = jnp.einsum("knr,ka->nra", back, jnp.asarray(inverse), preferred_element_type=F32)
    return denoised.astype(BF16)


def solution(mesh):
    placed = (P(("img", "grp"), None, None), P(("img", "grp")), P(), P(), P(), P())
    return jax.shard_map(
        body, mesh=mesh, in_specs=placed, out_specs=P(("img", "grp"), None, None), check_vma=False
    )
```

```python
import functools
import math

import jax
import jax.numpy as jnp
import numpy as np
from jax import lax
from jax.experimental import pallas as pl
from jax.experimental.pallas import tpu as pltpu
from jax.sharding import PartitionSpec as P

NS_ITERS = 7
SIDE = 4
MESH_ID = pl.DeviceIdType.MESH
F32 = jnp.float32
BF16 = jnp.bfloat16


def rem(a, n):
    return a % n if isinstance(a, int) else lax.rem(a, jnp.int32(n))


def div(a, n):
    return a // n if isinstance(a, int) else lax.div(a, jnp.int32(n))


def place():
    img = lax.axis_index("img")
    grp = lax.axis_index("grp")
    return div(grp, 2), div(img, 8), rem(img, 8), rem(grp, 2)


def owner_index(x, y, z):
    return x * 8 + y * 2 + rem(z, 2)


def step_of(i):
    turn = rem(i, 4)
    return rem(turn + 1, 4), rem(div(i, 4) + turn + 2, 4), rem(turn + div(i, 4) + div(i, 16) + 1, 2)


def peer_of(i, sign):
    x, y, z, core = place()
    a, b, c = step_of(i)
    px, py = rem(x + SIDE + sign * a, SIDE), rem(y + SIDE + sign * b, SIDE)
    pz = div(z, 2) * 2 + rem(z + c, 2)
    return {"img": py * 8 + pz, "grp": px * 2 + core}, owner_index(px, py, pz)


def lanes(shape):
    return lax.broadcasted_iota(jnp.int32, shape, len(shape) - 1)


def tile(index):
    return pl.ds(pl.multiple_of(index * 128, 128), 128)


def block_slots(counts, first):
    offsets, offset = [], 0
    for j in range(4):
        count = counts[first + j]
        offsets.append((offset, count))
        offset = offset + count
    return offsets


def slot_mask(lane, t, offset, count):
    slot = lane + t * 128
    return (slot >= offset) & (slot < offset + count)


def pack_block(counts, spectrum, basis, block, out):
    lane = lanes((64, 128))
    tiles = [jnp.zeros((64, 128), F32) for _ in range(3)]
    for j, (offset, count) in enumerate(block_slots(counts, block * 4)):
        freq = block * 4 + j
        rows = [spectrum[pl.ds(pl.multiple_of((c * 128 + freq) * 32, 32), 32), :] for c in range(2)]
        coeffs = jnp.dot(
            jnp.concatenate(rows, 0).astype(BF16), basis[freq], preferred_element_type=F32
        )
        turned = pltpu.roll(coeffs, offset % 128, 1)
        tiles = [
            jnp.where(slot_mask(lane, t, offset, count), turned, tiles[t]) for t in range(3)
        ]
    fold_slots(*tiles, out.at[block])


def fold_slots(low, middle, high, out):
    out[0:64] = low.astype(BF16)
    out[64:128] = middle.astype(BF16)
    lane = lanes((32, 128))
    out[128:160] = jnp.where(lane < 64, high[0:32], pltpu.roll(high[32:64], 64, 1)).astype(BF16)


def unfold_slots(high):
    lane = lanes((32, 128))
    high = high.astype(F32)
    first = jnp.where(lane < 64, high, 0.0)
    second = jnp.where(lane < 64, pltpu.roll(high, 64, 1), 0.0)
    return jnp.concatenate([first, second], 0)


def pick_slots(tiles, lane, offset, count):
    picked = jnp.zeros_like(tiles[0])
    for t in range(3):
        picked = jnp.where(slot_mask(lane, t, offset, count), tiles[t], picked)
    return pltpu.roll(picked, (128 - offset % 128) % 128, 1)


def unpack_block(counts, packed, basis, block, out, out_hbm, sent):
    lane = lanes((64, 128))
    tiles = [
        packed[block, 0:64].astype(F32),
        packed[block, 64:128].astype(F32),
        unfold_slots(packed[block, 128:160]),
    ]
    for j, (offset, count) in enumerate(block_slots(counts, block * 4)):
        freq = block * 4 + j
        cleaned = pick_slots(tiles, lane, offset, count).astype(BF16)
        back = lax.dot_general(
            cleaned, basis[freq], (((1,), (1,)), ((), ())), preferred_element_type=F32
        ).astype(BF16)
        for c in range(2):
            out[c * 128 + freq] = back[c * 32 : c * 32 + 32]
    for c in range(2):
        rows = pl.ds(c * 128 + block * 4, 4)
        pltpu.make_async_copy(out.at[rows], out_hbm.at[rows], sent).start()


def chunk_slots(packed, sources):
    rows = [packed[s] for s in sources]
    low = jnp.concatenate([r[0:64] for r in rows], 0).astype(F32)
    middle = jnp.concatenate([r[64:128] for r in rows], 0).astype(F32)
    high = jnp.concatenate([unfold_slots(r[128:160]) for r in rows], 0)
    return low, middle, high


def store_groups(all_ids, groups, sources):
    rows = jnp.concatenate([all_ids[s] for s in sources], 0).astype(F32)
    rows = jnp.concatenate([rows, jnp.zeros((4, 96), F32)], 1)
    turned = jnp.concatenate([rows, jnp.zeros((124, 128), F32)], 0).T[0:32]
    for i, s in enumerate(sources):
        groups[s] = jnp.broadcast_to(turned[:, i : i + 1], (32, 128))


def chunk_groups(groups, sources):
    return jnp.concatenate([r for s in sources for r in [groups[s]] * 2], 0)


def make_tables(slots, gains, first_freq, gram, table, member):
    gram[...] = jnp.zeros_like(gram)
    row = lax.broadcasted_iota(jnp.int32, (8, 512), 0)
    lane = lanes((8, 512))
    slot_gain = jnp.zeros((8, 512), F32)
    for j, (offset, count) in enumerate(slots):
        column = jnp.zeros((8, 512), F32)
        for g in range(8):
            column = jnp.where(row == g, gains[g, first_freq + j], column)
        here = ((lane >= offset) & (lane < offset + count)) | (lane == 384 + j)
        slot_gain = jnp.where(here, column, slot_gain)
    high = slot_gain.astype(BF16).astype(F32)
    middle = (slot_gain - high).astype(BF16).astype(F32)
    low = slot_gain - high - middle
    table[...] = jnp.concatenate([high, middle, low, jnp.zeros((104, 512), F32)], 0).astype(BF16)
    row = lax.broadcasted_iota(jnp.int32, (384, 128), 0)
    lane = lanes((384, 128))
    inside = jnp.zeros((384, 128), F32)
    for j, (offset, count) in enumerate(slots):
        inside = jnp.where((lane == j) & (row >= offset) & (row < offset + count), 1.0, inside)
    member[...] = inside.astype(BF16)


def add_chunk(packed, groups, sources, gram, table, member, sums):
    fourth, total = sums
    lane = lanes((256, 128))
    wanted = jnp.where(lane < 24, lane % 8, -1).astype(F32)
    value = jnp.concatenate(chunk_slots(packed, sources), 1)
    onehot = jnp.where(chunk_groups(groups, sources) == wanted, 1.0, 0.0).astype(BF16)
    gain = jnp.dot(onehot, table[...], preferred_element_type=F32)
    scaled = (value * gain[:, 0:384]).astype(BF16)
    products = lax.dot_general(
        scaled, scaled, (((0,), (0,)), ((), ())), preferred_element_type=F32
    )
    for t in range(3):
        gram[t, 0:384] += products[:, t * 128 : t * 128 + 128]
    square = value * value
    upper = square.astype(BF16)
    lower = (square - upper.astype(F32)).astype(BF16)
    norms = jnp.dot(upper, member[...], preferred_element_type=F32)
    norms += jnp.dot(lower, member[...], preferred_element_type=F32)
    weight = gain[:, 384:512] * gain[:, 384:512]
    fourth += jnp.sum(weight * norms * norms, 0, keepdims=True)
    total += jnp.sum(weight, 0, keepdims=True)
    return fourth, total


def gather_grams(slots, gram, sums, out):
    fourth, total = sums
    row = lax.broadcasted_iota(jnp.int32, (128, 128), 0)
    lane = lanes((128, 128))
    squares = []
    for offset, count in slots:
        tiles = [gram[t, pl.ds(offset, 128)] for t in range(3)]
        squares.append(jnp.where(row < count, pick_slots(tiles, lane, offset, count), 0.0))
    for half in range(2):
        upper, lower = squares[half * 2], squares[half * 2 + 1]
        out[half, 0:128] = jnp.where(row <= lane, upper, lower)
        diagonal = jnp.sum(jnp.where(row == lane, lower, 0.0), 0, keepdims=True)
        out[half, 128:136] = jnp.concatenate(
            [diagonal, fourth, total, jnp.zeros((5, 128), F32)], 0
        )


def split(value):
    high = value.astype(BF16)
    return high, (value - high.astype(F32)).astype(BF16)


def right_side(value):
    high, low = split(value)
    return jnp.concatenate(
        [jnp.concatenate([high, low], 1), jnp.concatenate([high, jnp.zeros_like(high)], 1)], 0
    )


def product(left, right):
    high, low = split(left)
    wide = jnp.dot(jnp.concatenate([high, low], 1), right, preferred_element_type=F32)
    return wide[:, 0:128] + wide[:, 128:256]


def total_of(value):
    return jnp.sum(jnp.sum(value, 0, keepdims=True), 1, keepdims=True)


def main_kernel(
    image_total, counts_in, gains_in, noise_in, images, basis_in, forward_in, ids_in, out_hbm,
    out, counts, gains, noise, forward, my_ids, pixels, spectrum, basis, packed, arrived, cleaned, returned, all_ids, groups, gram, table, member,
    part, other, mine, parts, cov_ref, cov_right, size, trace,
    my_filters, other_filters, shifted, filters, filters_last,
    local, load, load_basis, load_small, send, recv, send_ids, recv_ids, send_back, recv_back, send_sum, recv_sum,
):
    x, y, z, core = place()
    me = owner_index(x, y, z)
    quarter, low = z // 2, z % 2
    smalls = [(counts_in, counts), (gains_in, gains), (noise_in, noise)]
    smalls += [(forward_in, forward), (ids_in, my_ids)]
    smalls = [
        pltpu.make_async_copy(source, target, load_small.at[i])
        for i, (source, target) in enumerate(smalls)
    ]
    for copy in smalls:
        copy.start()

    def image_copy(m):
        rows = pl.ds(pl.multiple_of(m * 1024, 1024), 1024)
        return pltpu.make_async_copy(images.at[rows], pixels.at[rows], load.at[m])

    def basis_copy(m):
        freqs = pl.ds(m * 32, 32)
        return pltpu.make_async_copy(basis_in.at[freqs], basis.at[freqs], load_basis.at[m])

    for m in range(4):
        image_copy(m).start()
    for m in range(4):
        basis_copy(m).start()
    partner = {"img": y * 8 + z, "grp": x * 2 + 1 - core}
    column = []
    for step in (2, 1, 3):
        column.append({"img": y * 8 + (quarter + step) % 4 * 2 + low, "grp": x * 2 + core})
    barrier = pltpu.get_barrier_semaphore()
    for device in [peer_of(i, 1)[0] for i in range(31)] + [partner] + column:
        pl.semaphore_signal(barrier, inc=1, device_id=device, device_id_type=MESH_ID)
    for copy in smalls:
        copy.wait()
    slots = block_slots(counts, me * 4)

    def remote(source, target, sent, received, device):
        return pltpu.make_async_remote_copy(
            source, target, sent, received, device_id=device, device_id_type=MESH_ID
        )

    def data_copy(i):
        device, index = peer_of(i, 1)
        return remote(packed.at[index], arrived.at[me], send.at[i], recv.at[i], device)

    def ids_copy(i):
        return remote(my_ids, all_ids.at[me], send_ids.at[i], recv_ids.at[i], peer_of(i, 1)[0])

    def back_copy(i):
        device, index = peer_of(i, 1)
        return remote(cleaned.at[index], returned.at[me], send_back.at[i], recv_back.at[i], device)

    def sum_copy(source, target, i, device):
        return remote(source, target, send_sum.at[i], recv_sum.at[i], device)

    @pl.loop(0, 4)
    def _(m):
        image_copy(m).wait()
        rows = pl.ds(pl.multiple_of(m * 1024, 1024), 1024)
        lines = lax.dot_general(
            forward[...], pixels[rows, :], (((1,), (1,)), ((), ())), preferred_element_type=F32
        )
        for n in range(8):
            spectrum[pl.ds(m * 8 + n, 256, stride=32), :] = lines[:, n * 128 : n * 128 + 128]

    pl.semaphore_wait(barrier, 35)

    for m in range(4):
        basis_copy(m).wait()

    def send_block(i):
        ids_copy(i).start()
        data_copy(i).start()

    @pl.loop(0, 16)
    def _(pair):
        for half in range(2):
            pack_block(counts, spectrum, basis, peer_of(pair * 2 + half, 1)[1], packed)

        send_block(pair * 2)

        @pl.when(pair < 15)
        def _():
            send_block(pair * 2 + 1)

    own = pltpu.make_async_copy(packed.at[me], arrived.at[me], local.at[0])
    own.start()
    own_ids = pltpu.make_async_copy(my_ids, all_ids.at[me], local.at[1])
    own_ids.start()
    make_tables(slots, gains, me * 4, gram, table, member)
    own_ids.wait()
    own.wait()

    def chunk(m, sums):
        sources = []
        for s in range(4):
            i = m * 4 + s
            if s < 3:
                data_copy(i).wait_recv()
                ids_copy(i).wait_recv()
            else:

                @pl.when(i < 31)
                def _():
                    data_copy(i).wait_recv()
                    ids_copy(i).wait_recv()

            sources.append(peer_of(i, -1)[1])
        store_groups(all_ids, groups, sources)
        return add_chunk(arrived, groups, sources, gram, table, member, sums)

    nothing = jnp.zeros((1, 128), F32)
    gather_grams(slots, gram, lax.fori_loop(0, 8, chunk, (nothing, nothing)), part)

    swap = sum_copy(part.at[1 - core], other, 0, partner)
    swap.start()
    swap.wait()
    both = part[core] + other[...]
    mine[...] = both
    copies = [sum_copy(mine, parts.at[quarter], i + 1, d) for i, d in enumerate(column)]
    for copy in copies:
        copy.start()
    parts[quarter] = both
    shifted[...] = jnp.zeros_like(shifted)

    @pl.loop(0, 31)
    def _(i):
        ids_copy(i).wait_send()
        data_copy(i).wait_send()

    for copy in copies:
        copy.wait()
    make_covariances(image_total, counts, parts, cov_ref, cov_right, size, trace)

    def send_pair(pair):
        groups = pl.ds(pair * 2, 2)
        return sum_copy(my_filters.at[groups], other_filters.at[groups], pair + 4, partner)

    def place_pair(pair):
        for half in range(2):
            place_filters(
                slots, pair, half, my_filters, other_filters, shifted, filters, filters_last
            )

    @pl.loop(0, 2)
    def _(half):
        make_filters(half, gains, noise, my_filters, cov_ref, cov_right, size, trace)
        for pair in range(2):
            send_pair(half * 2 + pair).start()

    @pl.loop(0, 4)
    def _(pair):
        send_pair(pair).wait()
        place_pair(pair)

    @pl.loop(0, 8)
    def _(m):
        sources = [peer_of(m * 4 + s, 1)[1] for s in range(4)]
        apply_chunk(arrived, groups, sources, filters, filters_last, cleaned)
        for s in range(4):
            i = m * 4 + s
            if s < 3:
                back_copy(i).start()
            else:

                @pl.when(i < 31)
                def _():
                    back_copy(i).start()

    unpack_block(counts, cleaned, basis, me, out, out_hbm, local.at[2])

    @pl.loop(0, 15)
    def _(pair):
        for half in range(2):
            back_copy(pair * 2 + half).wait()
        for half in range(2):
            index = peer_of(pair * 2 + half, -1)[1]
            unpack_block(counts, returned, basis, index, out, out_hbm, local.at[2])

    back_copy(30).wait()
    unpack_block(counts, returned, basis, peer_of(30, -1)[1], out, out_hbm, local.at[2])
    pltpu.make_async_copy(out, out_hbm, local.at[2]).wait()


def make_covariances(images, counts, parts, cov_ref, cov_right, size, trace):
    x, y, z, core = place()
    first_freq = owner_index(x, y, z) * 4 + core * 2
    row = lax.broadcasted_iota(jnp.int32, (128, 128), 0)
    lane = lanes((128, 128))
    line = lanes((1, 128))
    block = ((parts[0] + parts[1]) + parts[2]) + parts[3]
    square = block[0:128]
    above = jnp.where(row < lane, square, 0.0)
    below = jnp.where(row > lane, square, 0.0)
    grams = (
        jnp.where(row <= lane, square, 0.0) + above.T,
        jnp.where(row == lane, block[128:129], below) + below.T,
    )
    for j in range(2):
        count = counts[first_freq + j]
        here = line == core * 2 + j
        fourth = jnp.sum(jnp.where(here, block[129:130], 0.0), 1, keepdims=True)
        total = jnp.sum(jnp.where(here, block[130:131], 0.0), 1, keepdims=True)
        sample = grams[j] / total
        ident = jnp.where((row == lane) & (row < count), 1.0, 0.0)
        level = total_of(sample * ident) / count.astype(F32)
        off_level = sample - level * ident
        spread = total_of(off_level * off_level)
        excess = (fourth / total - total_of(sample * sample)) / (2.0 * images)
        weight = excess / (excess + spread)
        cov = (1.0 - weight) * sample + (weight * level) * ident
        right = right_side(cov)
        square = product(cov, right)
        cov_ref[j, 0] = cov
        cov_ref[j, 1] = square
        cov_ref[j, 2] = product(square, right)
        cov_right[j] = right
        size[j] = jnp.broadcast_to(total_of(cov * cov), (8, 128))
        trace[j] = jnp.broadcast_to(total_of(cov * ident), (8, 128))


def make_filters(pair, gains, noise, out, cov_ref, cov_right, size, trace):
    x, y, z, core = place()
    first_freq = owner_index(x, y, z) * 4 + core * 2
    ident = jnp.where(
        lax.broadcasted_iota(jnp.int32, (128, 128), 0) == lanes((128, 128)), 1.0, 0.0
    )
    problems = [(pair * 4 + g, j) for g in range(4) for j in range(2)]
    powers, sums, scales = [], [], []
    for g, j in problems:
        gain, level = gains[g, first_freq + j], noise[first_freq + j]
        square = gain * gain
        norm = size[j, 0:1, 0:1] * (square * square)
        norm += trace[j, 0:1, 0:1] * (2.0 * square * level) + 128.0 * level * level
        scale = 1.0 / jnp.sqrt(norm)
        keep, slope = 1.0 - scale * level, scale * square
        first, second, third = cov_ref[j, 0], cov_ref[j, 1], cov_ref[j, 2]
        power = keep * ident - slope * first
        twice = keep * keep * ident - (2.0 * keep * slope) * first + slope * slope * second
        thrice = (
            keep * keep * keep * ident - (3.0 * keep * keep * slope) * first
            + (3.0 * keep * slope * slope) * second - slope * slope * slope * third
        )
        powers.append(twice)
        sums.append(ident + power + twice + thrice)
        scales.append(scale * gain)
    powers = [product(p, right_side(p)) for p in powers]
    for _ in range(NS_ITERS - 3):
        sides = [right_side(p) for p in powers]
        both = [product(jnp.concatenate([s, p], 0), r) for s, p, r in zip(sums, powers, sides)]
        sums = [s + b[0:128] for s, b in zip(sums, both)]
        powers = [b[128:256] for b in both]
    sums = [s + product(s, right_side(p)) for s, p in zip(sums, powers)]
    for (g, j), s, scale in zip(problems, sums, scales):
        out[g, j] = (scale * product(s, cov_right[j])).astype(BF16)


def place_filters(slots, pair, half, mine, other, shifted, filters, filters_last):
    g = pair * 2 + half
    core = place()[3]
    lane = lanes((128, 128))
    tiles = [[jnp.zeros((128, 128), F32)] * 3 for _ in range(3)]
    for j, (offset, count) in enumerate(slots):
        value = jnp.where(core == j // 2, mine[g, j % 2].astype(F32), other[g, j % 2].astype(F32))
        shifted[j, 128:256] = pltpu.roll(value, offset % 128, 1)
        for r in range(3):
            start = jnp.clip(r * 128 + 128 - offset, 0, 256)
            rows = shifted[j, pl.ds(start, 128)]
            for t in range(max(r - 1, 0), min(r + 2, 3)):
                tiles[r][t] = jnp.where(slot_mask(lane, t, offset, count), rows, tiles[r][t])
    for t in range(2):
        column = slice(t * 128, t * 128 + 128)
        for r in range(2):
            row = pl.ds(pl.multiple_of(g * 256 + r * 128, 128), 128)
            filters[row, column] = tiles[r][t].astype(BF16)
        filters[pl.ds(pl.multiple_of(2048 + pair * 128 + half * 64, 64), 64), column] = (
            tiles[2][t][0:64].astype(BF16)
        )
    filters_last[pl.ds(pl.multiple_of(g * 128, 128), 128), :] = tiles[1][2].astype(BF16)
    filters_last[pl.ds(pl.multiple_of(1024 + pair * 128 + half * 64, 64), 64), :] = (
        tiles[2][2][0:64].astype(BF16)
    )


def apply_chunk(packed, groups, sources, filters, filters_last, out):
    low, middle, high = chunk_slots(packed, sources)
    both = jnp.concatenate([low, middle], 1).astype(BF16)
    twice = (high + pltpu.roll(high, 64, 1)).astype(BF16)
    group = chunk_groups(groups, sources)
    second = jnp.where(lanes((256, 128)) >= 64, 1.0, 0.0)
    pieces, ends = [], []
    for g in range(8):
        mask = jnp.where(group == float(g), 1.0, 0.0).astype(BF16)
        pieces.append(both * jnp.concatenate([mask] * 2, 1))
    for pair in range(4):
        mask = jnp.where(group - second == float(pair * 2), 1.0, 0.0).astype(BF16)
        ends.append(twice * mask)
    left = jnp.concatenate(pieces + ends, 1)
    right = jnp.concatenate([p[:, 128:256] for p in pieces] + ends, 1)
    cleaned = jnp.concatenate(
        [
            jnp.dot(left, filters[...], preferred_element_type=F32),
            jnp.dot(right, filters_last[...], preferred_element_type=F32),
        ],
        1,
    )
    for s, source in enumerate(sources):
        rows = cleaned[s * 64 : s * 64 + 64]
        fold_slots(rows[:, 0:128], rows[:, 128:256], rows[:, 256:384], out.at[source])


def dft_tables(angles, freqs):
    angle_index, freq_index = np.arange(angles), np.arange(freqs)
    turns = angle_index[:, None] * freq_index[None, :] % angles
    phases = turns.astype(np.float32) * np.float32(2.0 * math.pi / angles)
    factor = np.float32(1.0 / math.sqrt(angles))
    cosine = np.cos(phases) * factor
    sine = -np.sin(phases) * factor
    doubling = np.where(freq_index == 0, 1.0, 2.0).astype(np.float32)
    forward = np.concatenate([cosine, sine], 1).T
    inverse = np.concatenate([cosine * doubling, sine * doubling], 1).T
    return forward.astype(BF16), inverse.astype(BF16)


def body(images, group_ids, counts, radial_basis, ctf_gain, noise_var):
    local_images, radii, angles = images.shape
    freqs = radial_basis.shape[0]
    image_total = local_images * lax.axis_size("img") * lax.axis_size("grp")
    dma = pltpu.SemaphoreType.DMA
    forward, inverse = dft_tables(angles, freqs)
    ids = group_ids.reshape(1, local_images)
    data = pltpu.VMEM((32, 160, 128), BF16)
    sums = pltpu.VMEM((136, 128), F32)
    pairs = pltpu.VMEM((8, 2, 128, 128), BF16)
    small = pltpu.VMEM((2, 8, 128), F32)
    hbm = pl.BlockSpec(memory_space=pltpu.HBM)
    back = pl.pallas_call(
        functools.partial(main_kernel, image_total),
        out_shape=jax.ShapeDtypeStruct((2 * freqs, local_images, radii), BF16),
        in_specs=[hbm] * 7,
        out_specs=hbm,
        scratch_shapes=[
            pltpu.VMEM((2 * freqs, local_images, radii), BF16),
            pltpu.SMEM(counts.shape, jnp.int32), pltpu.SMEM(ctf_gain.shape, F32),
            pltpu.SMEM(noise_var.shape, F32), pltpu.VMEM(forward.shape, BF16),
            pltpu.VMEM(ids.shape, jnp.int32),
            pltpu.VMEM((local_images * radii, angles), BF16),
            pltpu.VMEM((2 * freqs * local_images, radii), F32),
            pltpu.VMEM(radial_basis.shape, BF16),
            data, data, data, data,
            pltpu.VMEM((32, 1, 32), jnp.int32), pltpu.VMEM((32, 32, 128), F32),
            pltpu.VMEM((3, 512, 128), F32), pltpu.VMEM((128, 512), BF16),
            pltpu.VMEM((384, 128), BF16),
            pltpu.VMEM((2, 136, 128), F32), sums, sums, pltpu.VMEM((4, 136, 128), F32),
            pltpu.VMEM((2, 3, 128, 128), F32), pltpu.VMEM((2, 256, 256), BF16), small, small,
            pairs, pairs, pltpu.VMEM((4, 384, 128), F32), pltpu.VMEM((2560, 256), BF16),
            pltpu.VMEM((1536, 128), BF16),
            dma((3,)), dma((4,)), dma((4,)), dma((5,)),
            dma((31,)), dma((31,)), dma((31,)), dma((31,)), dma((31,)), dma((31,)),
            dma((8,)), dma((8,)),
        ],
        compiler_params=pltpu.CompilerParams(collective_id=0, has_side_effects=True),
        name="denoise",
    )(
        counts, ctf_gain, noise_var, images.reshape(local_images * radii, angles), radial_basis,
        jnp.asarray(forward), ids,
    )
    denoised = jnp.einsum("knr,ka->nra", back, jnp.asarray(inverse), preferred_element_type=F32)
    return denoised.astype(BF16)


def solution(mesh):
    placed = (P(("img", "grp"), None, None), P(("img", "grp")), P(), P(), P(), P())
    return jax.shard_map(
        body, mesh=mesh, in_specs=placed, out_specs=P(("img", "grp"), None, None), check_vma=False
    )
```
